512 devices in a mesh: chan: 16 (over y, core), tm: 32 (over z, x).
Axes of the slice: x: 4, y: 8, z: 8, core: 2. Of those that a mesh axis runs over, the one named last changes fastest.
Arguments:
- signal: float32 [256, 131072], P('chan', 'tm'), may hold values from -80 to 80
- filters: float32 [16, 131072], P(None, 'tm'), may hold values from -6 to 6
- gate_scale: float32 [256], P('chan'), may hold values from 0.5 to 2
- gate_shift: float32 [256], P('chan'), may hold values from -3 to 3
Outputs:
- predicted: float32 [256, 131072], P('chan', 'tm')
- grad_filter: float32 [16, 131072], P(None, 'tm')
- mean_loss: float32 [], replicated
The draws below stay inside these ranges and needn't reach their ends.
All inputs are finite; a program needn't handle non-finite values.
Results may differ from the reference program's by a relative error of at most 0.0003.
Values sent between devices are 32-bit elements; how exact they have to be, the bound alone decides.
A program may use at most 64 MiB of HBM per device.

```python
import math
import jax
import jax.numpy as jnp
from jax import lax

CHANNELS = 256
FILT = 16
LENGTH = 131072


def draw_signal(key, part):
    keys = jax.random.split(jax.random.fold_in(key, 17), 3)
    scales = jnp.exp(jax.random.uniform(keys[0], (CHANNELS, 1), minval=0.0, maxval=math.log(10.0)))
    slopes = jax.random.uniform(keys[1], (CHANNELS, 1), minval=-3.0, maxval=3.0)
    ramp = jnp.arange(LENGTH, dtype=jnp.float32)[None, :] / LENGTH
    noise = jax.random.truncated_normal(keys[2], -4.0, 4.0, (CHANNELS, LENGTH))
    values = scales * (noise + slopes * ramp)
    return values.astype(jnp.float32)


def steps_of(stream_key, dims, cuts, smallest, largest):
    loudness, own = 1.0, jax.random.fold_in(stream_key, 6)
    for dim, shards_of in cuts:
        heights = jnp.exp(jax.random.uniform(jax.random.fold_in(own, dim), (shards_of,), jnp.float32, smallest / len(cuts), largest / len(cuts)))
        loudness = loudness * jnp.repeat(heights, dims[dim] // shards_of).reshape([-1 if axis == dim else 1 for axis in range(len(dims))])
    return loudness


def bell_draw(rng, shape, scale, most, cuts=(), kind=jnp.bfloat16):
    drawn = jax.random.normal(rng, shape, jnp.float32) * scale
    if len(cuts) > 0:
        drawn = steps_of(rng, shape, cuts, -0.22, 0.18) * drawn
    return jnp.clip(drawn, min=-most, max=most).astype(kind)


def setup_inputs(seed: int = 0) -> dict:
    splits = jax.random.split(jax.random.key(seed), 5)
    signal = draw_signal(jax.random.fold_in(splits[4], 71), 0)
    filters = bell_draw(splits[1], (FILT, LENGTH), 1.0, 6.0, ((1, 32),), jnp.float32)
    gate_scale = jnp.clip(0.5 + 1.5 * jax.random.uniform(splits[2], (CHANNELS,), jnp.float32) ** steps_of(splits[2], (CHANNELS,), ((0, 16),), -0.2, 0.2), 0.5, 2.0)
    gate_shift = bell_draw(splits[3], (CHANNELS,), 1.0, 3.0, ((0, 16),), jnp.float32)
    return dict(signal=signal, filters=filters, gate_scale=gate_scale, gate_shift=gate_shift)


var_floor = 1.0

def reference(signal, filters, gate_scale, gate_shift):
    channels_all, full_length = signal.shape
    filter_count = filters.shape[0]
    groups_all = channels_all // filter_count
    counts = jnp.arange(1, full_length + 1).astype(jnp.float32)
    running_mean = jnp.cumsum(signal, axis=1) / counts
    running_var = jnp.cumsum(signal * signal, axis=1) / counts - running_mean * running_mean
    spread = jnp.sqrt(jnp.maximum(running_var, var_floor))
    normed = (signal - running_mean) / spread
    gating = jax.nn.sigmoid(gate_scale[:, None] * normed + gate_shift[:, None])
    padded_len = 2 * full_length
    tap_scale = 1.0 / jnp.sqrt(jnp.float32(full_length))
    taps = filters * tap_scale
    norm_spec = jnp.fft.rfft(normed, n=padded_len, axis=1).reshape(groups_all, filter_count, -1)
    filt_spec = jnp.fft.rfft(taps, n=padded_len, axis=1)
    mixed_conv = jnp.fft.irfft(norm_spec * filt_spec[None], n=padded_len, axis=2)[..., :full_length]
    mixed_conv = mixed_conv.reshape(channels_all, full_length).astype(jnp.float32)
    predicted = signal + spread * mixed_conv * gating
    target = jnp.concatenate([signal[:, 1:], jnp.zeros((channels_all, 1), jnp.float32)], axis=1)
    valid = jnp.arange(full_length) < full_length - 1
    residual = jnp.where(valid[None, :], predicted - target, 0.0)
    mean_loss = jnp.sum(residual * residual) / (channels_all * (full_length - 1))
    upstream = 2.0 / channels_all * residual * spread * gating
    up_spec = jnp.fft.rfft(upstream, n=padded_len, axis=1).reshape(groups_all, filter_count, -1)
    cross = lax.optimization_barrier(jnp.sum(up_spec * jnp.conj(norm_spec), axis=0))
    grad_filter = (jnp.fft.irfft(cross, n=padded_len, axis=1)[:, :full_length] * tap_scale).astype(jnp.float32)
    return (predicted, grad_filter, mean_loss)
```

```python
import math

import jax
import jax.numpy as jnp
import numpy as np
from jax import lax
from jax.experimental import pallas as pl
from jax.experimental.pallas import tpu as pltpu
from jax.sharding import PartitionSpec as P

CHANNELS = 256
LENGTH = 131072
N1, N2 = 512, 256
HALF = 256
SHARDS = 32
SEGS = 32
LANES = 128
var_floor = 1.0
MESH = pl.DeviceIdType.MESH
f32, bf16 = jnp.float32, jnp.bfloat16


def split_table(table):
    high = table.astype(np.float32).astype(bf16)
    low = (table - np.asarray(high).astype(np.float64)).astype(np.float32).astype(bf16)
    return np.asarray(high), np.asarray(low)


def make_tables():
    n1, n2 = np.arange(N1), np.arange(N2)
    k1 = np.arange(HALF)
    angle = 2 * math.pi * ((np.outer(4 * k1 + 1, n1) % (4 * N1)) / (4 * N1))
    outer = np.concatenate([np.cos(angle), -np.sin(angle)], axis=0)
    angle = 2 * math.pi * ((np.outer(n2, n2) % N2) / N2)
    inner = np.concatenate([np.cos(angle), np.sin(angle)], axis=1)
    angle = 2 * math.pi * (np.outer(4 * k1 + 1, n2) / (4 * LENGTH))
    twist = np.stack([np.cos(angle), -np.sin(angle)]).astype(np.float32)
    angle = math.pi * n2 / 256
    lane = np.zeros((8, N2), np.float32)
    lane[0], lane[1] = np.cos(angle), -np.sin(angle)
    return split_table(outer), split_table(outer.T), split_table(inner), twist, lane


def high_low(value):
    high = value.astype(bf16)
    return high, (value - high.astype(f32)).astype(bf16)


def three_way(value):
    high = value.astype(bf16)
    rest = value - high.astype(f32)
    middle = rest.astype(bf16)
    return high, middle, (rest - middle.astype(f32)).astype(bf16)


def dot(first, second):
    return jnp.dot(first, second, preferred_element_type=f32)


def kernel(
    signal, filters, scale_in, shift_in,
    outer_h, outer_l, outer_th, outer_tl, inner_h, inner_l, twist_hbm, lane_ref,
    pred_out, grad_out, loss_out,
    signal_send, filter_send, gate_send, gate_got,
    xbuf, fbuf, pbuf, ybuf, ygot, cbuf, cgot, rsbuf, rsum, prbuf, gbuf,
    loss_own, loss_mid, loss_sum, loss_all,
    outer_k, outer_tk, inner_k, twist,
    triple_x, triple_q, tri_up, tri_low, totals,
    spread_s, normed_s, gating_s, stack, left, spec_x, spec_f,
    table_sem, send_sem, recv_sem,
):
    group, at = lax.axis_index("chan"), lax.axis_index("tm")
    plane, core = group // 2, group % 2
    parity, owned = at % 2, at // 2
    filter_row = 2 * plane + parity
    partner = 2 * plane + 1 - core
    own_half = pl.multiple_of(core * 16, 16)

    def fetch(source, target, number):
        return pltpu.make_async_copy(source, target, table_sem.at[number])

    tables = [
        (outer_h, outer_k.at[:, pl.ds(0, N1)]), (outer_h, outer_k.at[:, pl.ds(N1, N1)]),
        (outer_l, outer_k.at[:, pl.ds(2 * N1, N1)]),
        (outer_th, outer_tk.at[:, pl.ds(0, N1)]), (outer_th, outer_tk.at[:, pl.ds(N1, N1)]),
        (outer_tl, outer_tk.at[:, pl.ds(2 * N1, N1)]),
        (inner_h, inner_k.at[pl.ds(0, N2)]), (inner_h, inner_k.at[pl.ds(N2, N2)]),
        (inner_l, inner_k.at[pl.ds(2 * N2, N2)]),
        (twist_hbm, twist),
    ]

    def remote(source, target, number, chan, tm):
        return pltpu.make_async_remote_copy(
            src_ref=source, dst_ref=target, send_sem=send_sem.at[number], recv_sem=recv_sem.at[number],
            device_id=(chan, tm), device_id_type=MESH,
        )

    def deliver(source, target, number, chan, tm):
        here = jnp.logical_and(chan == group, tm == at)

        @pl.when(jnp.logical_not(here))
        def _():
            remote(source, target, number, chan, tm).start()

        @pl.when(here)
        def _():
            pltpu.make_async_copy(source, target, recv_sem.at[number]).start()

    def arrived(target, number):
        pltpu.make_async_copy(target, target, recv_sem.at[number]).wait()

    def sent(source, number):
        pltpu.make_async_copy(source, source, send_sem.at[number]).wait()

    for seg in range(SEGS):
        signal_send[pl.ds(seg, 16, stride=SEGS), :] = signal[:, seg * LANES : (seg + 1) * LANES]
    signal_rows = signal_send.reshape(16, SEGS, LANES)

    def send_signal(step, carry):
        which = (step + at) % 32
        row, half = which // 2, which % 2
        part = pl.ds(pl.multiple_of(half * 16, 16), 16)
        deliver(
            signal_rows.at[row, part], xbuf.at[at, part], 0,
            2 * (row // 2) + half, 2 * group + row % 2,
        )
        return carry

    lax.fori_loop(0, 32, send_signal, 0)

    gate_send[0:1, 0:16] = scale_in[...]
    gate_send[1:2, 0:16] = shift_in[...]

    @pl.when(owned == group)
    def _():
        def send_gate(step, carry):
            deliver(gate_send, gate_got, 1, (group + step) % 16, at)
            return carry

        lax.fori_loop(0, 16, send_gate, 0)

    for seg in range(SEGS):
        filter_send[pl.ds(seg, 16, stride=SEGS), :] = filters[:, seg * LANES : (seg + 1) * LANES]
    filter_rows = filter_send.reshape(16, SEGS, LANES)

    def send_filter(step, carry):
        to = (step + at) % 32
        deliver(
            filter_rows.at[2 * plane + to % 2, pl.ds(own_half, 16)],
            fbuf.at[at, pl.ds(own_half, 16)], 2, group, to,
        )
        return carry

    lax.fori_loop(0, 32, send_filter, 0)

    for number, (source, target) in enumerate(tables):
        fetch(source, target, number).start()

    row_up = lax.broadcasted_iota(jnp.int32, (N2, N2), 0)
    col_up = lax.broadcasted_iota(jnp.int32, (N2, N2), 1)
    tri_up[...] = jnp.where(row_up <= col_up, 1.0, 0.0).astype(bf16)
    row_low = lax.broadcasted_iota(jnp.int32, (N1, N1), 0)
    col_low = lax.broadcasted_iota(jnp.int32, (N1, N1), 1)
    tri_low[...] = jnp.where(col_low < row_low, 1.0, 0.0).astype(bf16)

    for number, (source, target) in enumerate(tables):
        fetch(source, target, number).wait()
    core_f = core.astype(f32)
    lane_r = 1.0 + core_f * (lane_ref[0:1, :] - 1.0)
    lane_i = core_f * lane_ref[1:2, :]
    base_r, base_i = twist[0], twist[1]
    twist[0] = base_r * lane_r - base_i * lane_i
    twist[1] = base_r * lane_i + base_i * lane_r

    rows_here = lax.broadcasted_iota(jnp.int32, (32, 1), 0)
    flip = 1.0 - 2.0 * core_f * (rows_here % 2).astype(f32)
    all_rows = lax.broadcasted_iota(jnp.int32, (N1, 1), 0)
    flip_all = 1.0 - 2.0 * core_f * (all_rows % 2).astype(f32)

    x_lin = xbuf.reshape(SHARDS * SEGS, LANES)
    f_lin = fbuf.reshape(SHARDS * SEGS, LANES)
    p_lin = pbuf.reshape(SHARDS * SEGS, LANES)
    c_lin = cbuf.reshape(SHARDS * SEGS, LANES)

    def pair_rows(ref, q):
        base = pl.multiple_of(q * 64, 64)
        return jnp.concatenate(
            [ref[pl.ds(base, 32, stride=2), :], ref[pl.ds(base + 1, 32, stride=2), :]], axis=1
        )

    def put_pairs(ref, q, value):
        base = pl.multiple_of(q * 64, 64)
        ref[pl.ds(base, 32, stride=2), :] = value[:, :LANES]
        ref[pl.ds(base + 1, 32, stride=2), :] = value[:, LANES:]

    def rows(q, offset=0):
        return pl.ds(pl.multiple_of(q * 32 + offset, 32), 32)

    def fill_stack(q, value):
        high, low = high_low(value * flip)
        stack[rows(q), :] = high
        stack[rows(q, N1), :] = low
        stack[rows(q, 2 * N1), :] = high

    def fill_left(real, imag):
        for part, value in enumerate((real, imag)):
            high, low = high_low(value)
            place = slice(part * HALF, (part + 1) * HALF)
            left[place, 0:N2] = high
            left[place, N2 : 2 * N2] = low
            left[place, 2 * N2 : 3 * N2] = high

    def forward():
        first = dot(outer_k[...], stack[...])
        first_r, first_i = first[:HALF], first[HALF:]
        fill_left(first_r * twist[0] - first_i * twist[1], first_r * twist[1] + first_i * twist[0])
        quads = dot(left[...], inner_k[...])
        return quads[:HALF, :N2] + quads[HALF:, N2:], quads[HALF:, :N2] - quads[:HALF, N2:]

    def inverse(real, imag):
        fill_left(real, imag)
        quads = dot(left[...], inner_k[...])
        mid_r = quads[:HALF, :N2] - quads[HALF:, N2:]
        mid_i = quads[HALF:, :N2] + quads[:HALF, N2:]
        high, low = high_low(mid_r * twist[0] + mid_i * twist[1])
        stack[0:HALF, :] = high
        stack[N1 : N1 + HALF, :] = low
        stack[2 * N1 : 2 * N1 + HALF, :] = high
        high, low = high_low(mid_i * twist[0] - mid_r * twist[1])
        stack[HALF:N1, :] = high
        stack[N1 + HALF : 2 * N1, :] = low
        stack[2 * N1 + HALF : 3 * N1, :] = high
        return dot(outer_tk[...], stack[...]) * flip_all

    def swap(source, target, number):
        copy = remote(source, target, number, partner, at)
        copy.start()
        return copy

    arrived(xbuf.at[:, pl.ds(own_half, 16)], 0)
    copy = swap(xbuf.at[:, pl.ds(own_half, 16)], xbuf.at[:, pl.ds(own_half, 16)], 3)
    copy.wait()

    def split_rows(q, carry):
        value = pair_rows(x_lin, q)
        for part, piece in enumerate(three_way(value)):
            triple_x[rows(q, part * N1), :] = piece
        for part, piece in enumerate(three_way(value * value)):
            triple_q[rows(q, part * N1), :] = piece
        return carry

    lax.fori_loop(0, 16, split_rows, 0)
    sums = dot(triple_x[...], tri_up[...])
    normed_s[...] = sums[:N1] + sums[N1 : 2 * N1] + sums[2 * N1 :]
    sums = dot(triple_q[...], tri_up[...])
    spread_s[...] = sums[:N1] + sums[N1 : 2 * N1] + sums[2 * N1 :]
    row_sums = jnp.concatenate(
        [
            jnp.broadcast_to(normed_s[:, N2 - 1 : N2], (N1, LANES)),
            jnp.broadcast_to(spread_s[:, N2 - 1 : N2], (N1, LANES)),
        ],
        axis=1,
    )
    carried = dot(tri_low[...], jnp.concatenate(three_way(row_sums), axis=1))
    totals[...] = carried[:, :N2] + carried[:, N2 : 2 * N2] + carried[:, 2 * N2 :]

    arrived(gate_got, 1)
    pick = lax.broadcasted_iota(jnp.int32, (1, LANES), 1) == filter_row
    gate_gain = jnp.sum(jnp.where(pick, gate_got[0:1, :], 0.0), axis=1, keepdims=True)
    gate_bias = jnp.sum(jnp.where(pick, gate_got[1:2, :], 0.0), axis=1, keepdims=True)

    lane_index = lax.broadcasted_iota(jnp.int32, (32, N2), 1)
    row_index = lax.broadcasted_iota(jnp.int32, (32, N2), 0)

    def normalize(q, carry):
        value = pair_rows(x_lin, q)
        before = totals[rows(q), :]
        first = normed_s[rows(q), :] + jnp.concatenate([before[:, :LANES]] * 2, axis=1)
        second = spread_s[rows(q), :] + jnp.concatenate([before[:, LANES:]] * 2, axis=1)
        counts = ((q * 32 + row_index) * N2 + lane_index + 1).astype(f32)
        mean = first / counts
        variance = second / counts - mean * mean
        spread = jnp.sqrt(jnp.maximum(variance, var_floor))
        normed = (value - mean) / spread
        gating_s[rows(q), :] = 1.0 / (1.0 + jnp.exp(-(gate_gain * normed + gate_bias)))
        spread_s[rows(q), :] = spread
        fill_stack(q, normed)
        return carry

    lax.fori_loop(0, 16, normalize, 0)
    real, imag = forward()
    spec_x[0], spec_x[1] = real, imag

    arrived(fbuf.at[:, pl.ds(own_half, 16)], 2)
    copy = swap(fbuf.at[:, pl.ds(own_half, 16)], fbuf.at[:, pl.ds(own_half, 16)], 4)
    copy.wait()

    def take_filter(q, carry):
        fill_stack(q, pair_rows(f_lin, q))
        return carry

    lax.fori_loop(0, 16, take_filter, 0)
    real, imag = forward()
    factor = 1.0 / math.sqrt(LENGTH) / LENGTH
    real, imag = real * factor, imag * factor
    ybuf[...] = inverse(
        spec_x[0] * real - spec_x[1] * imag, spec_x[0] * imag + spec_x[1] * real
    )
    copy = swap(ybuf, ygot, 5)
    copy.wait()

    loss_own[...] = jnp.zeros((8, LANES), f32)

    def predict(q, carry):
        value = pair_rows(x_lin, q)
        opening = x_lin[pl.ds(pl.multiple_of(q * 64, 64), 32, stride=2), :][:, 0:1]
        after = jnp.minimum(q * 64 + 64, SHARDS * SEGS - 8)
        following = x_lin[pl.ds(pl.multiple_of(after, 8), 8), :][0:1, 0:1]
        edge = jnp.concatenate([opening[1:], following], axis=0)
        target = jnp.concatenate([value[:, 1:], edge], axis=1)
        weight = spread_s[rows(q), :] * gating_s[rows(q), :]
        own = ybuf[rows(q), :]
        other = ygot[rows(q), :]
        low_part = jnp.where(core == 0, own, other)
        high_part = jnp.where(core == 0, other, own)
        predicted = value + weight * (low_part + high_part)
        put_pairs(p_lin, q, predicted)
        step_index = (q * 32 + row_index) * N2 + lane_index
        residual = jnp.where(step_index < LENGTH - 1, predicted - target, 0.0)
        squares = residual * residual
        squares = squares[:, :LANES] + squares[:, LANES:]
        loss_own[...] += (squares[0:8] + squares[8:16]) + (squares[16:24] + squares[24:32])
        fill_stack(q, (2.0 / CHANNELS) * residual * weight)
        return carry

    lax.fori_loop(0, 16, predict, 0)

    def send_predicted(step, carry):
        to = (step + at) % 32
        deliver(
            pbuf.at[to, pl.ds(own_half, 16)], prbuf.at[filter_row, pl.ds(own_half, 16)], 6, owned, to
        )
        return carry

    lax.fori_loop(0, 32, send_predicted, 0)

    def send_loss(step, carry):
        deliver(loss_own, loss_mid.at[owned], 7, group, 2 * ((owned + step) % 16) + parity)
        return carry

    lax.fori_loop(0, 16, send_loss, 0)

    real, imag = forward()
    across_r = (real * spec_x[0] + imag * spec_x[1]) * factor
    across_i = (imag * spec_x[0] - real * spec_x[1]) * factor
    ybuf[...] = inverse(across_r, across_i)
    copy = swap(ybuf, cgot, 8)

    arrived(loss_mid, 7)
    loss_sum[...] = jnp.sum(loss_mid[...], axis=0)
    block = 2 * owned + core

    def send_loss_sum(step, carry):
        deliver(loss_sum, loss_all.at[filter_row], 9, (group + step) % 16, block)
        return carry

    lax.fori_loop(0, 16, send_loss_sum, 0)
    copy.wait()

    def add_halves(q, carry):
        put_pairs(c_lin, q, ybuf[rows(q), :] + cgot[rows(q), :])
        return carry

    lax.fori_loop(0, 16, add_halves, 0)

    def send_grad(step, carry):
        to = (owned + step) % 16
        deliver(cbuf.at[2 * to + core], rsbuf.at[owned], 10, group, 2 * to + parity)
        return carry

    lax.fori_loop(0, 16, send_grad, 0)
    arrived(rsbuf, 10)
    rsum[...] = jnp.sum(rsbuf[...], axis=0)

    def send_total(step, carry):
        deliver(rsum, gbuf.at[filter_row], 11, (group + step) % 16, block)
        return carry

    lax.fori_loop(0, 16, send_total, 0)

    arrived(prbuf, 6)
    pr_lin = prbuf.reshape(16 * SEGS, LANES)
    for seg in range(SEGS):
        pred_out[:, seg * LANES : (seg + 1) * LANES] = pr_lin[pl.ds(seg, 16, stride=SEGS), :]

    arrived(loss_all, 9)
    everything = jnp.sum(jnp.sum(loss_all[...], axis=0), keepdims=True)
    loss_out[...] = everything / (CHANNELS * (LENGTH - 1))

    arrived(gbuf, 11)
    g_lin = gbuf.reshape(16 * SEGS, LANES)
    for seg in range(SEGS):
        grad_out[:, seg * LANES : (seg + 1) * LANES] = g_lin[pl.ds(seg, 16, stride=SEGS), :]

    def drain(here, whole, less, number):
        @pl.when(here)
        def _():
            sent(less, number)

        @pl.when(jnp.logical_not(here))
        def _():
            sent(whole, number)

    own_row = owned == group
    drain(own_row, xbuf.at[pl.ds(0, 32), pl.ds(0, 16)], xbuf.at[pl.ds(0, 31), pl.ds(0, 16)], 0)

    @pl.when(own_row)
    def _():
        sent(loss_mid.at[pl.ds(0, 15)], 1)

    sent(xbuf.at[pl.ds(0, 31), pl.ds(0, 16)], 2)
    drain(own_row, xbuf.at[pl.ds(0, 32), pl.ds(0, 16)], xbuf.at[pl.ds(0, 31), pl.ds(0, 16)], 6)
    sent(loss_mid.at[pl.ds(0, 15)], 7)
    drain(core == parity, loss_mid.at[pl.ds(0, 16)], loss_mid.at[pl.ds(0, 15)], 9)
    sent(rsbuf.at[pl.ds(0, 15)], 10)
    drain(core == parity, rsbuf.at[pl.ds(0, 16)], rsbuf.at[pl.ds(0, 15)], 11)


def per_device(signal, filters, gate_scale, gate_shift):
    (outer_h, outer_l), (outer_th, outer_tl), (inner_h, inner_l), twist, lane = make_tables()
    vmem = pl.BlockSpec(memory_space=pltpu.VMEM)
    anywhere = pl.BlockSpec(memory_space=pl.ANY)

    def space(*shape, kind=f32):
        return pltpu.VMEM(shape, kind)

    predicted, grad, loss = pl.pallas_call(
        kernel,
        out_shape=(
            jax.ShapeDtypeStruct((16, 4096), f32),
            jax.ShapeDtypeStruct((16, 4096), f32),
            jax.ShapeDtypeStruct((1, 1), f32),
        ),
        in_specs=[vmem] * 4 + [anywhere] * 7 + [vmem],
        out_specs=(vmem, vmem, vmem),
        scratch_shapes=[
            space(512, LANES), space(512, LANES), space(8, LANES), space(8, LANES),
            space(SHARDS, SEGS, LANES), space(SHARDS, SEGS, LANES), space(SHARDS, SEGS, LANES),
            space(N1, N2), space(N1, N2), space(SHARDS, SEGS, LANES), space(N1, N2),
            space(16, SEGS, LANES), space(SEGS, LANES), space(16, SEGS, LANES), space(16, SEGS, LANES),
            space(8, LANES), space(16, 8, LANES), space(8, LANES), space(16, 8, LANES),
            space(N1, 3 * N1, kind=bf16), space(N1, 3 * N1, kind=bf16), space(3 * N2, 2 * N2, kind=bf16),
            space(2, HALF, N2),
            space(3 * N1, N2, kind=bf16), space(3 * N1, N2, kind=bf16),
            space(N2, N2, kind=bf16), space(N1, N1, kind=bf16), space(N1, N2),
            space(N1, N2), space(N1, N2), space(N1, N2), space(3 * N1, N2, kind=bf16),
            space(N1, 3 * N2, kind=bf16), space(2, HALF, N2), space(2, HALF, N2),
            pltpu.SemaphoreType.DMA((10,)), pltpu.SemaphoreType.DMA((12,)), pltpu.SemaphoreType.DMA((12,)),
        ],
        compiler_params=pltpu.CompilerParams(has_side_effects=True),
    )(
        signal, filters, gate_scale.reshape(1, 16), gate_shift.reshape(1, 16),
        outer_h, outer_l, outer_th, outer_tl, inner_h, inner_l, twist, lane,
    )
    return (predicted, grad, loss.reshape(()))


def solution(mesh):
    return jax.shard_map(
        per_device,
        mesh=mesh,
        in_specs=(P("chan", "tm"), P(None, "tm"), P("chan"), P("chan")),
        out_specs=(P("chan", "tm"), P(None, "tm"), P()),
        check_vma=False,
    )
```

```python
import math

import jax
import jax.numpy as jnp
import numpy as np
from jax import lax
from jax.experimental import pallas as pl
from jax.experimental.pallas import tpu as pltpu
from jax.sharding import PartitionSpec as P

CHANNELS = 256
LENGTH = 131072
N1, N2 = 512, 256
HALF = 256
SHARDS = 32
SEGS = 32
LANES = 128
var_floor = 1.0
MESH = pl.DeviceIdType.MESH
f32, bf16 = jnp.float32, jnp.bfloat16


def split_table(table):
    high = table.astype(np.float32).astype(bf16)
    low = (table - np.asarray(high).astype(np.float64)).astype(np.float32).astype(bf16)
    return np.asarray(high), np.asarray(low)


def make_tables():
    n1, n2 = np.arange(N1), np.arange(N2)
    k1 = np.arange(HALF)
    angle = 2 * math.pi * ((np.outer(4 * k1 + 1, n1) % (4 * N1)) / (4 * N1))
    outer = np.concatenate([np.cos(angle), -np.sin(angle)], axis=0)
    angle = 2 * math.pi * ((np.outer(n2, n2) % N2) / N2)
    inner = np.concatenate([np.cos(angle), np.sin(angle)], axis=1)
    angle = 2 * math.pi * (np.outer(4 * k1 + 1, n2) / (4 * LENGTH))
    twist = np.stack([np.cos(angle), -np.sin(angle)]).astype(np.float32)
    angle = math.pi * n2 / 256
    lane = np.zeros((8, N2), np.float32)
    lane[0], lane[1] = np.cos(angle), -np.sin(angle)
    return split_table(outer), split_table(outer.T), split_table(inner), twist, lane


def high_low(value):
    high = value.astype(bf16)
    return high, (value - high.astype(f32)).astype(bf16)


def three_way(value):
    high = value.astype(bf16)
    rest = value - high.astype(f32)
    middle = rest.astype(bf16)
    return high, middle, (rest - middle.astype(f32)).astype(bf16)


def dot(first, second):
    return jnp.dot(first, second, preferred_element_type=f32)


def kernel(
    signal, filters, scale_in, shift_in,
    outer_h, outer_l, outer_th, outer_tl, inner_h, inner_l, twist_hbm, lane_ref,
    pred_out, grad_out, loss_out,
    signal_send, filter_send, gate_send, gate_got,
    xbuf, fbuf, pbuf, ybuf, ygot, cbuf, cgot, csum, along_y, along_sum, across, across_sum,
    loss_acc, loss_own, loss_mid, loss_sum, loss_all,
    outer_k, outer_tk, inner_k, twist,
    triple_x, triple_q, tri_up, tri_low, totals,
    spread_s, normed_s, gating_s, stack, left, spec_x,
    table_sem, send_sem, recv_sem,
):
    group, at = lax.axis_index("chan"), lax.axis_index("tm")
    plane, core = group // 2, group % 2
    owner_core, owner_row = at % 2, at // 2
    partner = 2 * plane + 1 - core
    own_half = pl.ds(pl.multiple_of(core * 16, 16), 16)
    own_piece = pl.ds(pl.multiple_of((plane // 2) * 8, 8), 8)
    on_plane = plane % 2
    active = at % 2 == on_plane
    row_odd = owner_row % 2

    barrier = pltpu.get_barrier_semaphore()

    def greet(step, carry):
        other = (core * SHARDS + at + step) % (2 * SHARDS)
        pl.semaphore_signal(
            barrier, inc=1, device_id=(2 * plane + other // SHARDS, other % SHARDS), device_id_type=MESH
        )
        return carry

    lax.fori_loop(1, 2 * SHARDS, greet, 0)

    def greet_planes(step, carry):
        pl.semaphore_signal(
            barrier, inc=1, device_id=(2 * ((plane + step) % 8) + core, at), device_id_type=MESH
        )
        return carry

    lax.fori_loop(1, 8, greet_planes, 0)

    def fetch(source, target, number):
        return pltpu.make_async_copy(source, target, table_sem.at[number])

    tables = [
        (outer_h, outer_k.at[:, pl.ds(0, N1)]), (outer_h, outer_k.at[:, pl.ds(N1, N1)]),
        (outer_l, outer_k.at[:, pl.ds(2 * N1, N1)]),
        (outer_th, outer_tk.at[:, pl.ds(0, N1)]), (outer_th, outer_tk.at[:, pl.ds(N1, N1)]),
        (outer_tl, outer_tk.at[:, pl.ds(2 * N1, N1)]),
        (inner_h, inner_k.at[pl.ds(0, N2)]), (inner_h, inner_k.at[pl.ds(N2, N2)]),
        (inner_l, inner_k.at[pl.ds(2 * N2, N2)]),
        (twist_hbm, twist),
    ]
    for number, (source, target) in enumerate(tables):
        fetch(source, target, number).start()

    def remote(source, target, number, chan, tm):
        return pltpu.make_async_remote_copy(
            src_ref=source, dst_ref=target, send_sem=send_sem.at[number], recv_sem=recv_sem.at[number],
            device_id=(chan, tm), device_id_type=MESH,
        )

    def deliver(source, target, number, chan, tm):
        here = jnp.logical_and(chan == group, tm == at)

        @pl.when(jnp.logical_not(here))
        def _():
            remote(source, target, number, chan, tm).start()

        @pl.when(here)
        def _():
            pltpu.make_async_copy(source, target, recv_sem.at[number]).start()

    def arrived(target, number):
        pltpu.make_async_copy(target, target, recv_sem.at[number]).wait()

    def sent(source, number):
        pltpu.make_async_copy(source, source, send_sem.at[number]).wait()

    def swap(source, target, number):
        copy = remote(source, target, number, partner, at)
        copy.start()
        return copy

    for seg in range(SEGS):
        signal_send[pl.ds(seg, 16, stride=SEGS), :] = signal[:, seg * LANES : (seg + 1) * LANES]
    signal_rows = signal_send.reshape(16, SEGS, LANES)
    gate_send[...] = jnp.zeros((8, LANES), f32)
    gate_send[0:1, 0:16] = scale_in[...]
    gate_send[1:2, 0:16] = shift_in[...]
    for seg in range(SEGS):
        filter_send[pl.ds(seg, 16, stride=SEGS), :] = filters[:, seg * LANES : (seg + 1) * LANES]
    filter_rows = filter_send.reshape(16, SEGS, LANES)
    row_up = lax.broadcasted_iota(jnp.int32, (N2, N2), 0)
    col_up = lax.broadcasted_iota(jnp.int32, (N2, N2), 1)
    tri_up[...] = jnp.where(row_up <= col_up, 1.0, 0.0).astype(bf16)
    row_low = lax.broadcasted_iota(jnp.int32, (N1, N1), 0)
    col_low = lax.broadcasted_iota(jnp.int32, (N1, N1), 1)
    tri_low[...] = jnp.where(col_low < row_low, 1.0, 0.0).astype(bf16)

    pl.semaphore_wait(barrier, 2 * SHARDS - 1 + 7)

    def send_signal(step, carry):
        which = (step + at) % 32
        row, half = which // 2, which % 2
        part = pl.ds(pl.multiple_of(half * 16, 16), 16)
        deliver(
            signal_rows.at[row, part], xbuf.at[at, part], 0, 2 * plane + half, 2 * row + core
        )
        return carry

    lax.fori_loop(0, 32, send_signal, 0)
    gates = swap(gate_send, gate_got, 1)

    @pl.when(active)
    def _():
        def send_filter(step, carry):
            row = (step + owner_row) % 16
            deliver(
                filter_rows.at[row, own_piece], fbuf.at[at // 4, at % 4, own_piece], 2,
                2 * plane + row_odd, 2 * row + core,
            )
            return carry

        lax.fori_loop(0, 16, send_filter, 0)

    for number, (source, target) in enumerate(tables):
        fetch(source, target, number).wait()
    core_f = core.astype(f32)
    lane_r = 1.0 + core_f * (lane_ref[0:1, :] - 1.0)
    lane_i = core_f * lane_ref[1:2, :]
    base_r, base_i = twist[0], twist[1]
    twist[0] = base_r * lane_r - base_i * lane_i
    twist[1] = base_r * lane_i + base_i * lane_r

    rows_here = lax.broadcasted_iota(jnp.int32, (32, 1), 0)
    flip = 1.0 - 2.0 * core_f * (rows_here % 2).astype(f32)
    all_rows = lax.broadcasted_iota(jnp.int32, (N1, 1), 0)
    flip_all = 1.0 - 2.0 * core_f * (all_rows % 2).astype(f32)

    x_lin = xbuf.reshape(SHARDS * SEGS, LANES)
    f_lin = fbuf.reshape(SHARDS * SEGS, LANES)
    p_lin = pbuf.reshape(SHARDS * SEGS, LANES)
    c_lin = cbuf.reshape(SHARDS * SEGS, LANES)

    def pair_rows(ref, q):
        base = pl.multiple_of(q * 64, 64)
        return jnp.concatenate(
            [ref[pl.ds(base, 32, stride=2), :], ref[pl.ds(base + 1, 32, stride=2), :]], axis=1
        )

    def put_pairs(ref, q, value):
        base = pl.multiple_of(q * 64, 64)
        ref[pl.ds(base, 32, stride=2), :] = value[:, :LANES]
        ref[pl.ds(base + 1, 32, stride=2), :] = value[:, LANES:]

    def rows(q, offset=0):
        return pl.ds(pl.multiple_of(q * 32 + offset, 32), 32)

    def fill_stack(q, value):
        high, low = high_low(value * flip)
        stack[rows(q), :] = high
        stack[rows(q, N1), :] = low
        stack[rows(q, 2 * N1), :] = high

    def fill_left(real, imag):
        for part, value in enumerate((real, imag)):
            high, low = high_low(value)
            place = slice(part * HALF, (part + 1) * HALF)
            left[place, 0:N2] = high
            left[place, N2 : 2 * N2] = low
            left[place, 2 * N2 : 3 * N2] = high

    def forward():
        first = dot(outer_k[...], stack[...])
        first_r, first_i = first[:HALF], first[HALF:]
        fill_left(first_r * twist[0] - first_i * twist[1], first_r * twist[1] + first_i * twist[0])
        quads = dot(left[...], inner_k[...])
        return quads[:HALF, :N2] + quads[HALF:, N2:], quads[HALF:, :N2] - quads[:HALF, N2:]

    def inverse(real, imag):
        fill_left(real, imag)
        quads = dot(left[...], inner_k[...])
        mid_r = quads[:HALF, :N2] - quads[HALF:, N2:]
        mid_i = quads[HALF:, :N2] + quads[:HALF, N2:]
        high, low = high_low(mid_r * twist[0] + mid_i * twist[1])
        stack[0:HALF, :] = high
        stack[N1 : N1 + HALF, :] = low
        stack[2 * N1 : 2 * N1 + HALF, :] = high
        high, low = high_low(mid_i * twist[0] - mid_r * twist[1])
        stack[HALF:N1, :] = high
        stack[N1 + HALF : 2 * N1, :] = low
        stack[2 * N1 + HALF : 3 * N1, :] = high
        return dot(outer_tk[...], stack[...]) * flip_all

    own_blocks = fbuf.at[:, 2 * core + on_plane, own_piece]
    arrived(own_blocks, 2)

    def gather_filter(step, carry):
        remote(own_blocks, own_blocks, 3, 2 * ((plane + step) % 8) + core, at).start()
        return carry

    lax.fori_loop(1, 8, gather_filter, 0)
    arrived(xbuf.at[:, own_half], 0)
    copy = swap(xbuf.at[:, own_half], xbuf.at[:, own_half], 4)
    copy.wait()

    def split_rows(q, carry):
        value = pair_rows(x_lin, q)
        for part, piece in enumerate(three_way(value)):
            triple_x[rows(q, part * N1), :] = piece
        for part, piece in enumerate(three_way(value * value)):
            triple_q[rows(q, part * N1), :] = piece
        return carry

    lax.fori_loop(0, 16, split_rows, 0)
    sums = dot(triple_x[...], tri_up[...])
    normed_s[...] = sums[:N1] + sums[N1 : 2 * N1] + sums[2 * N1 :]
    sums = dot(triple_q[...], tri_up[...])
    spread_s[...] = sums[:N1] + sums[N1 : 2 * N1] + sums[2 * N1 :]
    row_sums = jnp.concatenate(
        [
            jnp.broadcast_to(normed_s[:, N2 - 1 : N2], (N1, LANES)),
            jnp.broadcast_to(spread_s[:, N2 - 1 : N2], (N1, LANES)),
        ],
        axis=1,
    )
    carried = dot(tri_low[...], jnp.concatenate(three_way(row_sums), axis=1))
    totals[...] = carried[:, :N2] + carried[:, N2 : 2 * N2] + carried[:, 2 * N2 :]

    gates.wait()
    gate_pair = jnp.where(core == owner_core, gate_send[...], gate_got[...])
    pick = lax.broadcasted_iota(jnp.int32, (1, LANES), 1) == owner_row
    gate_gain = jnp.sum(jnp.where(pick, gate_pair[0:1, :], 0.0), axis=1, keepdims=True)
    gate_bias = jnp.sum(jnp.where(pick, gate_pair[1:2, :], 0.0), axis=1, keepdims=True)

    lane_index = lax.broadcasted_iota(jnp.int32, (32, N2), 1)
    row_index = lax.broadcasted_iota(jnp.int32, (32, N2), 0)

    def normalize(q, carry):
        value = pair_rows(x_lin, q)
        before = totals[rows(q), :]
        first = normed_s[rows(q), :] + jnp.concatenate([before[:, :LANES]] * 2, axis=1)
        second = spread_s[rows(q), :] + jnp.concatenate([before[:, LANES:]] * 2, axis=1)
        counts = ((q * 32 + row_index) * N2 + lane_index + 1).astype(f32)
        mean = first / counts
        variance = second / counts - mean * mean
        spread = jnp.sqrt(jnp.maximum(variance, var_floor))
        normed = (value - mean) / spread
        gating_s[rows(q), :] = 1.0 / (1.0 + jnp.exp(-(gate_gain * normed + gate_bias)))
        spread_s[rows(q), :] = spread
        fill_stack(q, normed)
        return carry

    lax.fori_loop(0, 16, normalize, 0)
    arrived(xbuf.at[pl.ds(0, 14)], 3)
    core_blocks = fbuf.at[:, pl.ds(2 * core, 2)]
    copy = swap(core_blocks, core_blocks, 5)
    real, imag = forward()
    spec_x[0], spec_x[1] = real, imag
    copy.wait()

    def take_filter(q, carry):
        fill_stack(q, pair_rows(f_lin, q))
        return carry

    lax.fori_loop(0, 16, take_filter, 0)
    real, imag = forward()
    factor = 1.0 / math.sqrt(LENGTH) / LENGTH
    real, imag = real * factor, imag * factor
    ybuf[...] = inverse(
        spec_x[0] * real - spec_x[1] * imag, spec_x[0] * imag + spec_x[1] * real
    )
    copy = swap(ybuf, ygot, 6)
    copy.wait()

    loss_acc[...] = jnp.zeros((8, LANES), f32)

    def predict(q, carry):
        value = pair_rows(x_lin, q)
        opening = x_lin[pl.ds(pl.multiple_of(q * 64, 64), 32, stride=2), :][:, 0:1]
        after = jnp.minimum(q * 64 + 64, SHARDS * SEGS - 8)
        following = x_lin[pl.ds(pl.multiple_of(after, 8), 8), :][0:1, 0:1]
        edge = jnp.concatenate([opening[1:], following], axis=0)
        target = jnp.concatenate([value[:, 1:], edge], axis=1)
        weight = spread_s[rows(q), :] * gating_s[rows(q), :]
        predicted = value + weight * (ybuf[rows(q), :] + ygot[rows(q), :])
        put_pairs(p_lin, q, predicted)
        step_index = (q * 32 + row_index) * N2 + lane_index
        residual = jnp.where(step_index < LENGTH - 1, predicted - target, 0.0)
        squares = residual * residual
        squares = squares[:, :LANES] + squares[:, LANES:]
        loss_acc[...] += (squares[0:8] + squares[8:16]) + (squares[16:24] + squares[24:32])
        fill_stack(q, (2.0 / CHANNELS) * residual * weight)
        return carry

    lax.fori_loop(0, 16, predict, 0)

    def send_predicted(step, carry):
        to = (step + at) % 32
        deliver(
            pbuf.at[to, own_half], pred_out.at[owner_row, own_half], 7, 2 * plane + owner_core, to
        )
        return carry

    lax.fori_loop(0, 32, send_predicted, 0)
    loss_own[...] = jnp.sum(loss_acc[...], axis=0, keepdims=True)

    def send_loss(step, carry):
        deliver(loss_own, loss_mid.at[plane], 8, 2 * ((plane + step) % 8) + core, at)
        return carry

    lax.fori_loop(0, 8, send_loss, 0)

    real, imag = forward()
    across_r = (real * spec_x[0] + imag * spec_x[1]) * factor
    across_i = (imag * spec_x[0] - real * spec_x[1]) * factor
    local = inverse(across_r, across_i)
    c_lin[pl.ds(0, N1, stride=2), :] = local[:, :LANES]
    c_lin[pl.ds(1, N1, stride=2), :] = local[:, LANES:]
    copy = swap(cbuf.at[:, pl.ds(2 * (1 - core), 2)], cgot, 9)

    arrived(loss_mid, 8)
    loss_sum[...] = jnp.sum(loss_mid[...], axis=0)

    def send_loss_sum(step, carry):
        deliver(loss_sum, loss_all.at[at], 10, group, (at + step) % 32)
        return carry

    lax.fori_loop(0, 32, send_loss_sum, 0)
    copy.wait()
    csum[...] = cbuf[:, pl.ds(2 * core, 2)] + cgot[...]

    def send_along(step, carry):
        to = (plane + step) % 8
        piece = pl.ds(pl.multiple_of((to // 2) * 8, 8), 8)
        deliver(csum.at[:, to % 2, piece], along_y.at[plane], 11, 2 * to + core, at)
        return carry

    lax.fori_loop(0, 8, send_along, 0)
    arrived(along_y, 11)
    along_sum[...] = jnp.sum(along_y[...], axis=0)

    def send_across(step, carry):
        deliver(
            along_sum.at[step], across.at[owner_row // 2, owner_core], 12,
            2 * plane + row_odd, 4 * step + 2 * core + on_plane,
        )
        return carry

    lax.fori_loop(0, 8, send_across, 0)

    @pl.when(active)
    def _():
        arrived(across, 12)
        across_sum[...] = across[:, 0] + across[:, 1]

        def send_total(step, carry):
            deliver(across_sum, grad_out.at[:, core, own_piece], 13, 2 * ((plane + step) % 8) + core, at)
            return carry

        lax.fori_loop(0, 8, send_total, 0)

    arrived(loss_all, 10)
    everything = jnp.sum(jnp.sum(loss_all[...], axis=0), keepdims=True)
    loss_out[...] = everything / (CHANNELS * (LENGTH - 1))

    arrived(grad_out.at[:, core], 13)
    copy = swap(grad_out.at[:, core], grad_out.at[:, core], 14)

    def drain(less, whole, part, number):
        @pl.when(less)
        def _():
            sent(part, number)

        @pl.when(jnp.logical_not(less))
        def _():
            sent(whole, number)

    own_core = owner_core == core
    drain(own_core, xbuf.at[:, pl.ds(0, 16)], xbuf.at[pl.ds(0, 31), pl.ds(0, 16)], 0)

    @pl.when(active)
    def _():
        drain(
            jnp.logical_and(own_core, row_odd == core),
            xbuf.at[pl.ds(0, 16), pl.ds(0, 8)], xbuf.at[pl.ds(0, 15), pl.ds(0, 8)], 2,
        )
        sent(xbuf.at[pl.ds(0, 14)], 13)

    sent(xbuf.at[pl.ds(0, 14)], 3)
    drain(own_core, xbuf.at[:, pl.ds(0, 16)], xbuf.at[pl.ds(0, 31), pl.ds(0, 16)], 7)
    sent(loss_mid.at[pl.ds(0, 7)], 8)
    sent(loss_all.at[pl.ds(0, 31)], 10)
    sent(xbuf.at[pl.ds(0, 14)], 11)
    drain(
        jnp.logical_and(active, row_odd == core), along_sum, along_sum.at[pl.ds(0, 7)], 12
    )
    arrived(pred_out, 7)
    copy.wait()


def per_device(signal, filters, gate_scale, gate_shift):
    (outer_h, outer_l), (outer_th, outer_tl), (inner_h, inner_l), twist, lane = make_tables()
    vmem = pl.BlockSpec(memory_space=pltpu.VMEM)
    anywhere = pl.BlockSpec(memory_space=pl.ANY)

    def space(*shape, kind=f32):
        return pltpu.VMEM(shape, kind)

    predicted, grad, loss = pl.pallas_call(
        kernel,
        out_shape=(
            jax.ShapeDtypeStruct((16, SEGS, LANES), f32),
            jax.ShapeDtypeStruct((8, 2, SEGS, LANES), f32),
            jax.ShapeDtypeStruct((1, 1), f32),
        ),
        in_specs=[vmem] * 4 + [anywhere] * 7 + [vmem],
        out_specs=(anywhere, anywhere, vmem),
        scratch_shapes=[
            space(512, LANES), space(512, LANES), space(8, LANES), space(8, LANES),
            space(SHARDS, SEGS, LANES), space(8, 4, SEGS, LANES), space(SHARDS, SEGS, LANES),
            space(N1, N2), space(N1, N2), space(8, 4, SEGS, LANES), space(8, 2, SEGS, LANES),
            space(8, 2, SEGS, LANES), space(8, 8, 8, LANES), space(8, 8, LANES),
            space(8, 2, 8, LANES), space(8, 8, LANES),
            space(8, LANES), space(1, LANES), space(8, 1, LANES), space(1, LANES), space(32, 1, LANES),
            space(N1, 3 * N1, kind=bf16), space(N1, 3 * N1, kind=bf16), space(3 * N2, 2 * N2, kind=bf16),
            space(2, HALF, N2),
            space(3 * N1, N2, kind=bf16), space(3 * N1, N2, kind=bf16),
            space(N2, N2, kind=bf16), space(N1, N1, kind=bf16), space(N1, N2),
            space(N1, N2), space(N1, N2), space(N1, N2), space(3 * N1, N2, kind=bf16),
            space(N1, 3 * N2, kind=bf16), space(2, HALF, N2),
            pltpu.SemaphoreType.DMA((10,)), pltpu.SemaphoreType.DMA((15,)), pltpu.SemaphoreType.DMA((15,)),
        ],
        compiler_params=pltpu.CompilerParams(has_side_effects=True, collective_id=1),
    )(
        signal, filters, gate_scale.reshape(1, 16), gate_shift.reshape(1, 16),
        outer_h, outer_l, outer_th, outer_tl, inner_h, inner_l, twist, lane,
    )
    return (predicted.reshape(16, 4096), grad.reshape(16, 4096), loss.reshape(()))


def solution(mesh):
    return jax.shard_map(
        per_device,
        mesh=mesh,
        in_specs=(P("chan", "tm"), P(None, "tm"), P("chan"), P("chan")),
        out_specs=(P("chan", "tm"), P(None, "tm"), P()),
        check_vma=False,
    )
```

```python
import math

import jax
import jax.numpy as jnp
import numpy as np
from jax import lax
from jax.experimental import pallas as pl
from jax.experimental.pallas import tpu as pltpu
from jax.sharding import PartitionSpec as P

CHANNELS = 256
LENGTH = 131072
N1, N2 = 512, 256
HALF = 256
SHARDS = 32
SEGS = 32
LANES = 128
var_floor = 1.0
MESH = pl.DeviceIdType.MESH
FAR_FIRST = (4, 3, 5, 2, 6, 1, 7, 0)
f32, bf16 = jnp.float32, jnp.bfloat16


def split_table(table):
    high = table.astype(np.float32).astype(bf16)
    low = (table - np.asarray(high).astype(np.float64)).astype(np.float32).astype(bf16)
    return np.asarray(high), np.asarray(low)


def make_tables():
    n1, n2 = np.arange(N1), np.arange(N2)
    k1 = np.arange(HALF)
    angle = 2 * math.pi * ((np.outer(4 * k1 + 1, n1) % (4 * N1)) / (4 * N1))
    outer = np.concatenate([np.cos(angle), -np.sin(angle)], axis=0)
    angle = 2 * math.pi * ((np.outer(n2, n2) % N2) / N2)
    inner = np.concatenate([np.cos(angle), np.sin(angle)], axis=1)
    angle = 2 * math.pi * (np.outer(4 * k1 + 1, n2) / (4 * LENGTH))
    twist = np.stack([np.cos(angle), -np.sin(angle)]).astype(np.float32)
    angle = math.pi * n2 / 256
    lane = np.zeros((8, N2), np.float32)
    lane[0], lane[1] = np.cos(angle), -np.sin(angle)
    return split_table(outer), split_table(outer.T), split_table(inner), twist, lane


def high_low(value):
    high = value.astype(bf16)
    return high, (value - high.astype(f32)).astype(bf16)


def three_way(value):
    high = value.astype(bf16)
    rest = value - high.astype(f32)
    middle = rest.astype(bf16)
    return high, middle, (rest - middle.astype(f32)).astype(bf16)


def dot(first, second):
    return jnp.dot(first, second, preferred_element_type=f32)


def kernel(
    signal, filters, scale_in, shift_in,
    outer_h, outer_l, outer_th, outer_tl, inner_h, inner_l, twist_hbm, lane_ref,
    pred_out, grad_out, loss_out,
    signal_send, filter_send, gate_send, gate_got,
    xbuf, fbuf, pbuf, ybuf, ygot, cbuf, cgot, csum, along_y, along_sum, across, across_sum,
    loss_acc, loss_own, loss_mid, loss_sum, loss_all,
    outer_k, outer_tk, inner_k, twist,
    triple_x, triple_q, tri_up, tri_low, totals,
    spread_s, normed_s, gating_s, stack, left, spec_x,
    table_sem, send_sem, recv_sem,
):
    group, at = lax.axis_index("chan"), lax.axis_index("tm")
    plane, core = group // 2, group % 2
    owner_core, owner_row = at % 2, at // 2
    depth, width = at // 4, at % 4
    partner = 2 * plane + 1 - core
    own_half = pl.ds(pl.multiple_of(core * 16, 16), 16)
    own_piece = pl.ds(pl.multiple_of((plane // 2) * 8, 8), 8)
    on_plane = plane % 2
    active = at % 2 == on_plane
    row_odd = owner_row % 2

    barrier = pltpu.get_barrier_semaphore()

    def greet(step, carry):
        other = (core * SHARDS + at + step) % (2 * SHARDS)
        pl.semaphore_signal(
            barrier, inc=1, device_id=(2 * plane + other // SHARDS, other % SHARDS), device_id_type=MESH
        )
        return carry

    lax.fori_loop(1, 2 * SHARDS, greet, 0)

    def greet_planes(step, carry):
        pl.semaphore_signal(
            barrier, inc=1, device_id=(2 * ((plane + step) % 8) + core, at), device_id_type=MESH
        )
        return carry

    lax.fori_loop(1, 8, greet_planes, 0)

    def fetch(source, target, number):
        return pltpu.make_async_copy(source, target, table_sem.at[number])

    tables = [
        (outer_h, outer_k.at[:, pl.ds(0, N1)]), (outer_h, outer_k.at[:, pl.ds(N1, N1)]),
        (outer_l, outer_k.at[:, pl.ds(2 * N1, N1)]),
        (outer_th, outer_tk.at[:, pl.ds(0, N1)]), (outer_th, outer_tk.at[:, pl.ds(N1, N1)]),
        (outer_tl, outer_tk.at[:, pl.ds(2 * N1, N1)]),
        (inner_h, inner_k.at[pl.ds(0, N2)]), (inner_h, inner_k.at[pl.ds(N2, N2)]),
        (inner_l, inner_k.at[pl.ds(2 * N2, N2)]),
        (twist_hbm, twist),
    ]
    for number, (source, target) in enumerate(tables):
        fetch(source, target, number).start()

    def remote(source, target, number, chan, tm):
        return pltpu.make_async_remote_copy(
            src_ref=source, dst_ref=target, send_sem=send_sem.at[number], recv_sem=recv_sem.at[number],
            device_id=(chan, tm), device_id_type=MESH,
        )

    def deliver(source, target, number, chan, tm):
        here = jnp.logical_and(chan == group, tm == at)

        @pl.when(jnp.logical_not(here))
        def _():
            remote(source, target, number, chan, tm).start()

        @pl.when(here)
        def _():
            pltpu.make_async_copy(source, target, recv_sem.at[number]).start()

    def arrived(target, number):
        pltpu.make_async_copy(target, target, recv_sem.at[number]).wait()

    def sent(source, number):
        pltpu.make_async_copy(source, source, send_sem.at[number]).wait()

    def swap(source, target, number):
        copy = remote(source, target, number, partner, at)
        copy.start()
        return copy

    for seg in range(SEGS):
        signal_send[pl.ds(seg, 16, stride=SEGS), :] = signal[:, seg * LANES : (seg + 1) * LANES]
    signal_rows = signal_send.reshape(16, SEGS, LANES)
    gate_send[...] = jnp.zeros((8, LANES), f32)
    gate_send[0:1, 0:16] = scale_in[...]
    gate_send[1:2, 0:16] = shift_in[...]
    for seg in range(SEGS):
        filter_send[pl.ds(seg, 16, stride=SEGS), :] = filters[:, seg * LANES : (seg + 1) * LANES]
    filter_rows = filter_send.reshape(16, SEGS, LANES)
    row_up = lax.broadcasted_iota(jnp.int32, (N2, N2), 0)
    col_up = lax.broadcasted_iota(jnp.int32, (N2, N2), 1)
    tri_up[...] = jnp.where(row_up <= col_up, 1.0, 0.0).astype(bf16)
    def rows(q, offset=0):
        return pl.ds(pl.multiple_of(q * 32 + offset, 32), 32)

    row_low = lax.broadcasted_iota(jnp.int32, (32, N1), 0)
    col_low = lax.broadcasted_iota(jnp.int32, (32, N1), 1)

    def fill_low(q, carry):
        tri_low[rows(q), :] = jnp.where(col_low < row_low + q * 32, 1.0, 0.0).astype(bf16)
        return carry

    lax.fori_loop(0, 16, fill_low, 0)
    pl.semaphore_wait(barrier, 2 * SHARDS - 1 + 7)

    @pl.when(active)
    def _():
        for far in FAR_FIRST:
            for side in (0, 1):
                row = 2 * ((depth + far) % 8) + side
                deliver(
                    filter_rows.at[row, own_piece], fbuf.at[depth, width, own_piece], 2,
                    2 * plane + row_odd, 2 * row + core,
                )

    for far in FAR_FIRST:
        for side in (0, 1):
            row = 2 * ((depth + far) % 8) + side
            for half in (0, 1):
                part = pl.ds(half * 16, 16)
                deliver(
                    signal_rows.at[row, part], xbuf.at[at, part], 0, 2 * plane + half, 2 * row + core
                )
    gates = swap(gate_send, gate_got, 1)

    for number, (source, target) in enumerate(tables):
        fetch(source, target, number).wait()
    core_f = core.astype(f32)
    lane_r = 1.0 + core_f * (lane_ref[0:1, :] - 1.0)
    lane_i = core_f * lane_ref[1:2, :]
    base_r, base_i = twist[0], twist[1]
    twist[0] = base_r * lane_r - base_i * lane_i
    twist[1] = base_r * lane_i + base_i * lane_r

    rows_here = lax.broadcasted_iota(jnp.int32, (32, 1), 0)
    flip = 1.0 - 2.0 * core_f * (rows_here % 2).astype(f32)
    half_rows = lax.broadcasted_iota(jnp.int32, (HALF, 1), 0)
    flip_half = 1.0 - 2.0 * core_f * (half_rows % 2).astype(f32)

    x_lin = xbuf.reshape(SHARDS * SEGS, LANES)
    f_lin = fbuf.reshape(SHARDS * SEGS, LANES)
    p_lin = pbuf.reshape(SHARDS * SEGS, LANES)
    c_lin = cbuf.reshape(SHARDS * SEGS, LANES)

    def pair_rows(ref, q):
        base = pl.multiple_of(q * 64, 64)
        return jnp.concatenate(
            [ref[pl.ds(base, 32, stride=2), :], ref[pl.ds(base + 1, 32, stride=2), :]], axis=1
        )

    def put_pairs(ref, q, value):
        base = pl.multiple_of(q * 64, 64)
        ref[pl.ds(base, 32, stride=2), :] = value[:, :LANES]
        ref[pl.ds(base + 1, 32, stride=2), :] = value[:, LANES:]

    def fill_stack(q, value):
        high, low = high_low(value * flip)
        stack[rows(q), :] = high
        stack[rows(q, N1), :] = low
        stack[rows(q, 2 * N1), :] = high

    def fill_left(real, imag):
        for part, value in enumerate((real, imag)):
            high, low = high_low(value)
            place = slice(part * HALF, (part + 1) * HALF)
            left[place, 0:N2] = high
            left[place, N2 : 2 * N2] = low
            left[place, 2 * N2 : 3 * N2] = high

    def forward():
        first = dot(outer_k[...], stack[...])
        first_r, first_i = first[:HALF], first[HALF:]
        fill_left(first_r * twist[0] - first_i * twist[1], first_r * twist[1] + first_i * twist[0])
        quads = dot(left[...], inner_k[...])
        return quads[:HALF, :N2] + quads[HALF:, N2:], quads[HALF:, :N2] - quads[:HALF, N2:]

    def inverse(real, imag, take):
        fill_left(real, imag)
        quads = dot(left[...], inner_k[...])
        mid_r = quads[:HALF, :N2] - quads[HALF:, N2:]
        mid_i = quads[HALF:, :N2] + quads[:HALF, N2:]
        high, low = high_low(mid_r * twist[0] + mid_i * twist[1])
        stack[0:HALF, :] = high
        stack[N1 : N1 + HALF, :] = low
        stack[2 * N1 : 2 * N1 + HALF, :] = high
        high, low = high_low(mid_i * twist[0] - mid_r * twist[1])
        stack[HALF:N1, :] = high
        stack[N1 + HALF : 2 * N1, :] = low
        stack[2 * N1 + HALF : 3 * N1, :] = high
        for half in (0, 1):
            place = slice(half * HALF, (half + 1) * HALF)
            take(half, dot(outer_tk[place, :], stack[...]) * flip_half)

    own_blocks = fbuf.at[:, 2 * core + on_plane, own_piece]
    arrived(own_blocks, 2)

    for far in FAR_FIRST[:-1]:
        remote(own_blocks, own_blocks, 3, 2 * ((plane + far) % 8) + core, at).start()
    arrived(xbuf.at[:, own_half], 0)
    copy = swap(xbuf.at[:, own_half], xbuf.at[:, own_half], 4)
    copy.wait()

    def split_rows(q, carry):
        value = pair_rows(x_lin, q)
        for part, piece in enumerate(three_way(value)):
            triple_x[rows(q, part * N1), :] = piece
        for part, piece in enumerate(three_way(value * value)):
            triple_q[rows(q, part * N1), :] = piece
        return carry

    lax.fori_loop(0, 16, split_rows, 0)
    sums = dot(triple_x[...], tri_up[...])
    normed_s[...] = sums[:N1] + sums[N1 : 2 * N1] + sums[2 * N1 :]
    sums = dot(triple_q[...], tri_up[...])
    spread_s[...] = sums[:N1] + sums[N1 : 2 * N1] + sums[2 * N1 :]
    row_sums = jnp.concatenate(
        [
            jnp.broadcast_to(normed_s[:, N2 - 1 : N2], (N1, LANES)),
            jnp.broadcast_to(spread_s[:, N2 - 1 : N2], (N1, LANES)),
        ],
        axis=1,
    )
    carried = dot(tri_low[...], jnp.concatenate(three_way(row_sums), axis=1))
    totals[...] = carried[:, :N2] + carried[:, N2 : 2 * N2] + carried[:, 2 * N2 :]

    gates.wait()
    gate_pair = jnp.where(core == owner_core, gate_send[...], gate_got[...])
    pick = lax.broadcasted_iota(jnp.int32, (1, LANES), 1) == owner_row
    gate_gain = jnp.sum(jnp.where(pick, gate_pair[0:1, :], 0.0), axis=1, keepdims=True)
    gate_bias = jnp.sum(jnp.where(pick, gate_pair[1:2, :], 0.0), axis=1, keepdims=True)

    lane_index = lax.broadcasted_iota(jnp.int32, (32, N2), 1)
    row_index = lax.broadcasted_iota(jnp.int32, (32, N2), 0)

    def normalize(q, carry):
        value = pair_rows(x_lin, q)
        before = totals[rows(q), :]
        first = normed_s[rows(q), :] + jnp.concatenate([before[:, :LANES]] * 2, axis=1)
        second = spread_s[rows(q), :] + jnp.concatenate([before[:, LANES:]] * 2, axis=1)
        counts = ((q * 32 + row_index) * N2 + lane_index + 1).astype(f32)
        mean = first / counts
        variance = second / counts - mean * mean
        spread = jnp.sqrt(jnp.maximum(variance, var_floor))
        normed = (value - mean) / spread
        gating_s[rows(q), :] = 1.0 / (1.0 + jnp.exp(-(gate_gain * normed + gate_bias)))
        spread_s[rows(q), :] = spread
        fill_stack(q, normed)
        return carry

    lax.fori_loop(0, 16, normalize, 0)
    arrived(xbuf.at[pl.ds(0, 14)], 3)
    core_blocks = fbuf.at[:, pl.ds(2 * core, 2)]
    copy = swap(core_blocks, core_blocks, 5)
    real, imag = forward()
    spec_x[0], spec_x[1] = real, imag
    copy.wait()

    def take_filter(q, carry):
        fill_stack(q, pair_rows(f_lin, q))
        return carry

    lax.fori_loop(0, 16, take_filter, 0)
    real, imag = forward()
    factor = 1.0 / math.sqrt(LENGTH) / LENGTH
    real, imag = real * factor, imag * factor
    copies = []

    def exchange(half, value):
        place = pl.ds(half * HALF, HALF)
        ybuf[place, :] = value
        copies.append(swap(ybuf.at[place], ygot.at[place], 6 + 9 * half))

    inverse(
        spec_x[0] * real - spec_x[1] * imag, spec_x[0] * imag + spec_x[1] * real, exchange
    )

    loss_acc[...] = jnp.zeros((8, LANES), f32)

    def predict(q, carry):
        value = pair_rows(x_lin, q)
        opening = x_lin[pl.ds(pl.multiple_of(q * 64, 64), 32, stride=2), :][:, 0:1]
        after = jnp.minimum(q * 64 + 64, SHARDS * SEGS - 8)
        following = x_lin[pl.ds(pl.multiple_of(after, 8), 8), :][0:1, 0:1]
        edge = jnp.concatenate([opening[1:], following], axis=0)
        target = jnp.concatenate([value[:, 1:], edge], axis=1)
        weight = spread_s[rows(q), :] * gating_s[rows(q), :]
        predicted = value + weight * (ybuf[rows(q), :] + ygot[rows(q), :])
        put_pairs(p_lin, q, predicted)
        step_index = (q * 32 + row_index) * N2 + lane_index
        residual = jnp.where(step_index < LENGTH - 1, predicted - target, 0.0)
        squares = residual * residual
        squares = squares[:, :LANES] + squares[:, LANES:]
        loss_acc[...] += (squares[0:8] + squares[8:16]) + (squares[16:24] + squares[24:32])
        fill_stack(q, (2.0 / CHANNELS) * residual * weight)
        return carry

    copies[0].wait()
    lax.fori_loop(0, 8, predict, 0)
    copies[1].wait()
    lax.fori_loop(8, 16, predict, 0)

    def send_predicted(step, carry):
        to = (step + at + 14) % 32
        deliver(
            pbuf.at[to, own_half], pred_out.at[owner_row, own_half], 7, 2 * plane + owner_core, to
        )
        return carry

    lax.fori_loop(0, 32, send_predicted, 0)
    loss_own[...] = jnp.sum(loss_acc[...], axis=0, keepdims=True)

    def send_loss(step, carry):
        deliver(loss_own, loss_mid.at[plane], 8, 2 * ((plane + step) % 8) + core, at)
        return carry

    lax.fori_loop(0, 8, send_loss, 0)

    real, imag = forward()
    across_r = (real * spec_x[0] + imag * spec_x[1]) * factor
    across_i = (imag * spec_x[0] - real * spec_x[1]) * factor
    copies = []

    def exchange_grad(half, value):
        base, place = half * N1, pl.ds(half * 4, 4)
        c_lin[pl.ds(base, HALF, stride=2), :] = value[:, :LANES]
        c_lin[pl.ds(base + 1, HALF, stride=2), :] = value[:, LANES:]
        copies.append(swap(cbuf.at[place, pl.ds(2 * (1 - core), 2)], cgot.at[place], 9 + 7 * half))

    inverse(across_r, across_i, exchange_grad)

    for half in (0, 1):
        copies[half].wait()
        place = pl.ds(half * 4, 4)
        csum[place] = cbuf[place, pl.ds(2 * core, 2)] + cgot[place]
        for far in FAR_FIRST:
            to = (plane + far) % 8
            piece = pl.ds(pl.multiple_of((to // 2) * 8, 8), 8)
            deliver(
                csum.at[place, to % 2, piece], along_y.at[half, plane], 11 + 6 * half, 2 * to + core, at
            )

    arrived(loss_mid, 8)
    loss_sum[...] = jnp.sum(loss_mid[...], axis=0)

    def send_loss_sum(step, carry):
        deliver(loss_sum, loss_all.at[at], 10, group, (at + step) % 32)
        return carry

    lax.fori_loop(0, 32, send_loss_sum, 0)

    for half in (0, 1):
        arrived(along_y.at[half], 11 + 6 * half)
        along_sum[pl.ds(half * 4, 4)] = jnp.sum(along_y[half], axis=0)
        for step in range(half * 4, half * 4 + 4):
            deliver(
                along_sum.at[step], across.at[owner_row // 2, owner_core], 12,
                2 * plane + row_odd, 4 * step + 2 * core + on_plane,
            )

    @pl.when(active)
    def _():
        arrived(across, 12)
        across_sum[...] = across[:, 0] + across[:, 1]

        for far in FAR_FIRST:
            deliver(
                across_sum, grad_out.at[:, core, own_piece], 13, 2 * ((plane + far) % 8) + core, at
            )

    arrived(loss_all, 10)
    everything = jnp.sum(jnp.sum(loss_all[...], axis=0), keepdims=True)
    loss_out[...] = everything / (CHANNELS * (LENGTH - 1))

    arrived(grad_out.at[:, core], 13)
    copy = swap(grad_out.at[:, core], grad_out.at[:, core], 14)

    def drain(less, whole, part, number):
        @pl.when(less)
        def _():
            sent(part, number)

        @pl.when(jnp.logical_not(less))
        def _():
            sent(whole, number)

    own_core = owner_core == core
    drain(own_core, xbuf.at[:, pl.ds(0, 16)], xbuf.at[pl.ds(0, 31), pl.ds(0, 16)], 0)

    @pl.when(active)
    def _():
        drain(
            jnp.logical_and(own_core, row_odd == core),
            xbuf.at[pl.ds(0, 16), pl.ds(0, 8)], xbuf.at[pl.ds(0, 15), pl.ds(0, 8)], 2,
        )
        sent(xbuf.at[pl.ds(0, 14)], 13)

    sent(xbuf.at[pl.ds(0, 14)], 3)
    drain(own_core, xbuf.at[:, pl.ds(0, 16)], xbuf.at[pl.ds(0, 31), pl.ds(0, 16)], 7)
    sent(loss_mid.at[pl.ds(0, 7)], 8)
    sent(loss_all.at[pl.ds(0, 31)], 10)
    sent(xbuf.at[pl.ds(0, 7)], 11)
    sent(xbuf.at[pl.ds(0, 7)], 17)
    drain(
        jnp.logical_and(active, row_odd == core), along_sum, along_sum.at[pl.ds(0, 7)], 12
    )
    arrived(pred_out, 7)
    copy.wait()


def per_device(signal, filters, gate_scale, gate_shift):
    (outer_h, outer_l), (outer_th, outer_tl), (inner_h, inner_l), twist, lane = make_tables()
    vmem = pl.BlockSpec(memory_space=pltpu.VMEM)
    anywhere = pl.BlockSpec(memory_space=pl.ANY)

    def space(*shape, kind=f32):
        return pltpu.VMEM(shape, kind)

    predicted, grad, loss = pl.pallas_call(
        kernel,
        out_shape=(
            jax.ShapeDtypeStruct((16, SEGS, LANES), f32),
            jax.ShapeDtypeStruct((8, 2, SEGS, LANES), f32),
            jax.ShapeDtypeStruct((1, 1), f32),
        ),
        in_specs=[vmem] * 4 + [anywhere] * 7 + [vmem],
        out_specs=(anywhere, anywhere, vmem),
        scratch_shapes=[
            space(512, LANES), space(512, LANES), space(8, LANES), space(8, LANES),
            space(SHARDS, SEGS, LANES), space(8, 4, SEGS, LANES), space(SHARDS, SEGS, LANES),
            space(N1, N2), space(N1, N2), space(8, 4, SEGS, LANES), space(8, 2, SEGS, LANES),
            space(8, 2, SEGS, LANES), space(2, 8, 4, 8, LANES), space(8, 8, LANES),
            space(8, 2, 8, LANES), space(8, 8, LANES),
            space(8, LANES), space(1, LANES), space(8, 1, LANES), space(1, LANES), space(32, 1, LANES),
            space(N1, 3 * N1, kind=bf16), space(N1, 3 * N1, kind=bf16), space(3 * N2, 2 * N2, kind=bf16),
            space(2, HALF, N2),
            space(3 * N1, N2, kind=bf16), space(3 * N1, N2, kind=bf16),
            space(N2, N2, kind=bf16), space(N1, N1, kind=bf16), space(N1, N2),
            space(N1, N2), space(N1, N2), space(N1, N2), space(3 * N1, N2, kind=bf16),
            space(N1, 3 * N2, kind=bf16), space(2, HALF, N2),
            pltpu.SemaphoreType.DMA((10,)), pltpu.SemaphoreType.DMA((18,)), pltpu.SemaphoreType.DMA((18,)),
        ],
        compiler_params=pltpu.CompilerParams(has_side_effects=True, collective_id=1),
    )(
        signal, filters, gate_scale.reshape(1, 16), gate_shift.reshape(1, 16),
        outer_h, outer_l, outer_th, outer_tl, inner_h, inner_l, twist, lane,
    )
    return (predicted.reshape(16, 4096), grad.reshape(16, 4096), loss.reshape(()))


def solution(mesh):
    return jax.shard_map(
        per_device,
        mesh=mesh,
        in_specs=(P("chan", "tm"), P(None, "tm"), P("chan"), P("chan")),
        out_specs=(P("chan", "tm"), P(None, "tm"), P()),
        check_vma=False,
    )
```

```python
import math

import jax
import jax.numpy as jnp
import numpy as np
from jax import lax
from jax.experimental import pallas as pl
from jax.experimental.pallas import tpu as pltpu
from jax.sharding import PartitionSpec as P

CHANNELS = 256
LENGTH = 131072
N1, N2 = 512, 256
HALF = 256
SHARDS = 32
SEGS = 32
LANES = 128
var_floor = 1.0
MESH = pl.DeviceIdType.MESH
FAR_FIRST = (4, 3, 5, 2, 6, 1, 7, 0)
f32, bf16 = jnp.float32, jnp.bfloat16


def split_table(table):
    high = table.astype(np.float32).astype(bf16)
    low = (table - np.asarray(high).astype(np.float64)).astype(np.float32).astype(bf16)
    return np.asarray(high), np.asarray(low)


def make_tables():
    n1, n2 = np.arange(N1), np.arange(N2)
    k1 = np.arange(HALF)
    angle = 2 * math.pi * ((np.outer(4 * k1 + 1, n1) % (4 * N1)) / (4 * N1))
    outer = np.concatenate([np.cos(angle), -np.sin(angle)], axis=0)
    angle = 2 * math.pi * ((np.outer(n2, n2) % N2) / N2)
    inner = np.concatenate([np.cos(angle), np.sin(angle)], axis=1)
    angle = 2 * math.pi * (np.outer(4 * k1 + 1, n2) / (4 * LENGTH))
    twist = np.stack([np.cos(angle), -np.sin(angle)]).astype(np.float32)
    angle = math.pi * n2 / 256
    lane = np.zeros((8, N2), np.float32)
    lane[0], lane[1] = np.cos(angle), -np.sin(angle)
    return split_table(outer), split_table(outer.T), split_table(inner), twist, lane


def high_low(value):
    high = value.astype(bf16)
    return high, (value - high.astype(f32)).astype(bf16)


def three_way(value):
    high = value.astype(bf16)
    rest = value - high.astype(f32)
    middle = rest.astype(bf16)
    return high, middle, (rest - middle.astype(f32)).astype(bf16)


def dot(first, second):
    return jnp.dot(first, second, preferred_element_type=f32)


def kernel(
    signal_hbm, filters_hbm, scale_in, shift_in,
    outer_h, outer_l, outer_th, outer_tl, inner_h, inner_l, twist_hbm, lane_ref,
    pred_out, grad_out, loss_out,
    signal, filters, signal_send, filter_send, gate_send, gate_got,
    xbuf, fbuf, pbuf, ybuf, ygot, cbuf, cgot, csum, along_y, along_sum, across, across_sum,
    loss_acc, loss_own, loss_mid, loss_sum, loss_all,
    outer_k, outer_tk, inner_k, twist,
    triple_x, triple_q, tri_up, tri_low, totals,
    spread_s, normed_s, gating_s, stack, left, spec_x,
    table_sem, send_sem, recv_sem,
):
    group, at = lax.axis_index("chan"), lax.axis_index("tm")
    plane, core = group // 2, group % 2
    owner_core, owner_row = at % 2, at // 2
    depth, width = at // 4, at % 4
    partner = 2 * plane + 1 - core
    own_half = pl.ds(pl.multiple_of(core * 16, 16), 16)
    own_piece = pl.ds(pl.multiple_of((plane // 2) * 8, 8), 8)
    on_plane = plane % 2
    active = at % 2 == on_plane
    row_odd = owner_row % 2

    barrier = pltpu.get_barrier_semaphore()

    def greet(chan, tm):
        pl.semaphore_signal(barrier, inc=1, device_id=(chan, tm), device_id_type=MESH)

    for far in FAR_FIRST[:-1]:
        for step in range(8):
            greet(2 * plane + step % 2, 4 * ((depth + far) % 8) + step // 2)
    for far in FAR_FIRST[:-1]:
        greet(2 * ((plane + far) % 8) + core, at)
    for side in (2, 1, 3):
        for step in (0, 1):
            greet(2 * plane + step, 4 * depth + (width + side) % 4)
    greet(partner, at)

    def fetch(source, target, number):
        return pltpu.make_async_copy(source, target, table_sem.at[number])

    tables = [
        (outer_h, outer_k.at[:, pl.ds(0, N1)]), (outer_h, outer_k.at[:, pl.ds(N1, N1)]),
        (outer_l, outer_k.at[:, pl.ds(2 * N1, N1)]),
        (outer_th, outer_tk.at[:, pl.ds(0, N1)]), (outer_th, outer_tk.at[:, pl.ds(N1, N1)]),
        (outer_tl, outer_tk.at[:, pl.ds(2 * N1, N1)]),
        (inner_h, inner_k.at[pl.ds(0, N2)]), (inner_h, inner_k.at[pl.ds(N2, N2)]),
        (inner_l, inner_k.at[pl.ds(2 * N2, N2)]),
        (twist_hbm, twist),
    ]
    own_taps = pl.ds(pl.multiple_of((plane // 2) * 1024, 1024), 1024)
    inputs = [(signal_hbm, signal), (filters_hbm.at[:, own_taps], filters)]
    for number, (source, target) in enumerate(inputs):
        fetch(source, target, 10 + number).start()
    for number, (source, target) in enumerate(tables):
        fetch(source, target, number).start()

    def remote(source, target, number, chan, tm):
        return pltpu.make_async_remote_copy(
            src_ref=source, dst_ref=target, send_sem=send_sem.at[number], recv_sem=recv_sem.at[number],
            device_id=(chan, tm), device_id_type=MESH,
        )

    def deliver(source, target, number, chan, tm):
        here = jnp.logical_and(chan == group, tm == at)

        @pl.when(jnp.logical_not(here))
        def _():
            remote(source, target, number, chan, tm).start()

        @pl.when(here)
        def _():
            pltpu.make_async_copy(source, target, recv_sem.at[number]).start()

    def arrived(target, number):
        pltpu.make_async_copy(target, target, recv_sem.at[number]).wait()

    def sent(source, number):
        pltpu.make_async_copy(source, source, send_sem.at[number]).wait()

    def swap(source, target, number):
        copy = remote(source, target, number, partner, at)
        copy.start()
        return copy

    def signal_turn(seg, carry):
        signal_send[pl.ds(seg, 16, stride=SEGS), :] = signal[:, pl.ds(pl.multiple_of(seg * LANES, LANES), LANES)]
        return carry

    fetch(*inputs[0], 10).wait()
    lax.fori_loop(0, SEGS, signal_turn, 0, unroll=4)
    signal_rows = signal_send.reshape(16, SEGS, LANES)
    gate_send[...] = jnp.zeros((8, LANES), f32)
    gate_send[0:1, 0:16] = scale_in[...]
    gate_send[1:2, 0:16] = shift_in[...]
    fetch(*inputs[1], 11).wait()
    for seg in range(8):
        filter_send[pl.ds(seg, 16, stride=8), :] = filters[:, seg * LANES : (seg + 1) * LANES]
    filter_rows = filter_send.reshape(16, 8, LANES)

    pl.semaphore_wait(barrier, 2 * SHARDS - 1 + 7)

    @pl.when(active)
    def _():
        for far in FAR_FIRST:
            for side in (0, 1):
                row = 2 * ((depth + far) % 8) + side
                deliver(
                    filter_rows.at[row], fbuf.at[depth, width, own_piece], 2,
                    2 * plane + row_odd, 2 * row + core,
                )

    for far in FAR_FIRST:
        for side in (0, 1):
            row = 2 * ((depth + far) % 8) + side
            for half in (0, 1):
                part = pl.ds(half * 16, 16)
                deliver(
                    signal_rows.at[row, part], xbuf.at[at, part], 0, 2 * plane + half, 2 * row + core
                )
    gates = swap(gate_send, gate_got, 1)

    row_up = lax.broadcasted_iota(jnp.int32, (N2, N2), 0)
    col_up = lax.broadcasted_iota(jnp.int32, (N2, N2), 1)
    tri_up[...] = jnp.where(row_up <= col_up, 1.0, 0.0).astype(bf16)

    def rows(q, offset=0):
        return pl.ds(pl.multiple_of(q * 32 + offset, 32), 32)

    row_low = lax.broadcasted_iota(jnp.int32, (32, N1), 0)
    col_low = lax.broadcasted_iota(jnp.int32, (32, N1), 1)

    def fill_low(q, carry):
        tri_low[rows(q), :] = jnp.where(col_low < row_low + q * 32, 1.0, 0.0).astype(bf16)
        return carry

    lax.fori_loop(0, 16, fill_low, 0)

    for number, (source, target) in enumerate(tables):
        fetch(source, target, number).wait()
    core_f = core.astype(f32)
    lane_r = 1.0 + core_f * (lane_ref[0:1, :] - 1.0)
    lane_i = core_f * lane_ref[1:2, :]
    base_r, base_i = twist[0], twist[1]
    twist[0] = base_r * lane_r - base_i * lane_i
    twist[1] = base_r * lane_i + base_i * lane_r

    rows_here = lax.broadcasted_iota(jnp.int32, (32, 1), 0)
    flip = 1.0 - 2.0 * core_f * (rows_here % 2).astype(f32)
    half_rows = lax.broadcasted_iota(jnp.int32, (HALF, 1), 0)
    flip_half = 1.0 - 2.0 * core_f * (half_rows % 2).astype(f32)

    x_lin = xbuf.reshape(SHARDS * SEGS, LANES)
    f_lin = fbuf.reshape(SHARDS * SEGS, LANES)
    p_lin = pbuf.reshape(SHARDS * SEGS, LANES)
    c_lin = cbuf.reshape(SHARDS * SEGS, LANES)

    def pair_rows(ref, q):
        base = pl.multiple_of(q * 64, 64)
        return jnp.concatenate(
            [ref[pl.ds(base, 32, stride=2), :], ref[pl.ds(base + 1, 32, stride=2), :]], axis=1
        )

    def put_pairs(ref, q, value):
        base = pl.multiple_of(q * 64, 64)
        ref[pl.ds(base, 32, stride=2), :] = value[:, :LANES]
        ref[pl.ds(base + 1, 32, stride=2), :] = value[:, LANES:]

    def fill_stack(q, value):
        high, low = high_low(value * flip)
        stack[rows(q), :] = high
        stack[rows(q, N1), :] = low
        stack[rows(q, 2 * N1), :] = high

    def fill_left(real, imag):
        for part, value in enumerate((real, imag)):
            high, low = high_low(value)
            place = slice(part * HALF, (part + 1) * HALF)
            left[place, 0:N2] = high
            left[place, N2 : 2 * N2] = low
            left[place, 2 * N2 : 3 * N2] = high

    def forward():
        first = dot(outer_k[...], stack[...])
        first_r, first_i = first[:HALF], first[HALF:]
        fill_left(first_r * twist[0] - first_i * twist[1], first_r * twist[1] + first_i * twist[0])
        quads = dot(left[...], inner_k[...])
        return quads[:HALF, :N2] + quads[HALF:, N2:], quads[HALF:, :N2] - quads[:HALF, N2:]

    def inverse(real, imag, take):
        fill_left(real, imag)
        quads = dot(left[...], inner_k[...])
        mid_r = quads[:HALF, :N2] - quads[HALF:, N2:]
        mid_i = quads[HALF:, :N2] + quads[:HALF, N2:]
        high, low = high_low(mid_r * twist[0] + mid_i * twist[1])
        stack[0:HALF, :] = high
        stack[N1 : N1 + HALF, :] = low
        stack[2 * N1 : 2 * N1 + HALF, :] = high
        high, low = high_low(mid_i * twist[0] - mid_r * twist[1])
        stack[HALF:N1, :] = high
        stack[N1 + HALF : 2 * N1, :] = low
        stack[2 * N1 + HALF : 3 * N1, :] = high
        for half in (0, 1):
            place = slice(half * HALF, (half + 1) * HALF)
            take(half, dot(outer_tk[place, :], stack[...]) * flip_half)

    own_blocks = fbuf.at[:, 2 * core + on_plane, own_piece]
    arrived(own_blocks, 2)

    for far in FAR_FIRST[:-1]:
        remote(own_blocks, own_blocks, 3, 2 * ((plane + far) % 8) + core, at).start()
    arrived(xbuf.at[:, own_half], 0)
    copy = swap(xbuf.at[:, own_half], xbuf.at[:, own_half], 4)
    copy.wait()

    def split_rows(q, carry):
        value = pair_rows(x_lin, q)
        for part, piece in enumerate(three_way(value)):
            triple_x[rows(q, part * N1), :] = piece
        for part, piece in enumerate(three_way(value * value)):
            triple_q[rows(q, part * N1), :] = piece
        return carry

    lax.fori_loop(0, 16, split_rows, 0, unroll=2)
    sums = dot(triple_x[...], tri_up[...])
    normed_s[...] = sums[:N1] + sums[N1 : 2 * N1] + sums[2 * N1 :]
    sums = dot(triple_q[...], tri_up[...])
    spread_s[...] = sums[:N1] + sums[N1 : 2 * N1] + sums[2 * N1 :]
    row_sums = jnp.concatenate(
        [
            jnp.broadcast_to(normed_s[:, N2 - 1 : N2], (N1, LANES)),
            jnp.broadcast_to(spread_s[:, N2 - 1 : N2], (N1, LANES)),
        ],
        axis=1,
    )
    carried = dot(tri_low[...], jnp.concatenate(three_way(row_sums), axis=1))
    totals[...] = carried[:, :N2] + carried[:, N2 : 2 * N2] + carried[:, 2 * N2 :]

    gates.wait()
    gate_pair = jnp.where(core == owner_core, gate_send[...], gate_got[...])
    pick = lax.broadcasted_iota(jnp.int32, (1, LANES), 1) == owner_row
    gate_gain = jnp.sum(jnp.where(pick, gate_pair[0:1, :], 0.0), axis=1, keepdims=True)
    gate_bias = jnp.sum(jnp.where(pick, gate_pair[1:2, :], 0.0), axis=1, keepdims=True)

    lane_index = lax.broadcasted_iota(jnp.int32, (32, N2), 1)
    row_index = lax.broadcasted_iota(jnp.int32, (32, N2), 0)

    def normalize(q, carry):
        value = pair_rows(x_lin, q)
        before = totals[rows(q), :]
        first = normed_s[rows(q), :] + jnp.concatenate([before[:, :LANES]] * 2, axis=1)
        second = spread_s[rows(q), :] + jnp.concatenate([before[:, LANES:]] * 2, axis=1)
        counts = ((q * 32 + row_index) * N2 + lane_index + 1).astype(f32)
        mean = first / counts
        variance = second / counts - mean * mean
        spread = jnp.sqrt(jnp.maximum(variance, var_floor))
        normed = (value - mean) / spread
        gating_s[rows(q), :] = 1.0 / (1.0 + jnp.exp(-(gate_gain * normed + gate_bias)))
        spread_s[rows(q), :] = spread
        fill_stack(q, normed)
        return carry

    lax.fori_loop(0, 16, normalize, 0, unroll=2)
    arrived(xbuf.at[pl.ds(0, 14)], 3)
    core_blocks = fbuf.at[:, pl.ds(2 * core, 2)]
    copy = swap(core_blocks, core_blocks, 5)
    real, imag = forward()
    spec_x[0], spec_x[1] = real, imag
    copy.wait()

    def take_filter(q, carry):
        fill_stack(q, pair_rows(f_lin, q))
        return carry

    lax.fori_loop(0, 16, take_filter, 0, unroll=2)
    real, imag = forward()
    factor = 1.0 / math.sqrt(LENGTH) / LENGTH
    real, imag = real * factor, imag * factor
    copies = []

    def exchange(half, value):
        place = pl.ds(half * HALF, HALF)
        ybuf[place, :] = value
        copies.append(swap(ybuf.at[place], ygot.at[place], 6 + 9 * half))

    inverse(
        spec_x[0] * real - spec_x[1] * imag, spec_x[0] * imag + spec_x[1] * real, exchange
    )

    loss_acc[...] = jnp.zeros((8, LANES), f32)

    def predict(q, carry):
        value = pair_rows(x_lin, q)
        opening = x_lin[pl.ds(pl.multiple_of(q * 64, 64), 32, stride=2), :][:, 0:1]
        after = jnp.minimum(q * 64 + 64, SHARDS * SEGS - 8)
        following = x_lin[pl.ds(pl.multiple_of(after, 8), 8), :][0:1, 0:1]
        edge = jnp.concatenate([opening[1:], following], axis=0)
        target = jnp.concatenate([value[:, 1:], edge], axis=1)
        weight = spread_s[rows(q), :] * gating_s[rows(q), :]
        predicted = value + weight * (ybuf[rows(q), :] + ygot[rows(q), :])
        put_pairs(p_lin, q, predicted)
        step_index = (q * 32 + row_index) * N2 + lane_index
        residual = jnp.where(step_index < LENGTH - 1, predicted - target, 0.0)
        squares = residual * residual
        squares = squares[:, :LANES] + squares[:, LANES:]
        loss_acc[...] += (squares[0:8] + squares[8:16]) + (squares[16:24] + squares[24:32])
        fill_stack(q, (2.0 / CHANNELS) * residual * weight)
        return carry

    copies[0].wait()
    lax.fori_loop(0, 8, predict, 0, unroll=2)
    copies[1].wait()
    lax.fori_loop(8, 16, predict, 0, unroll=2)

    real, imag = forward()
    across_r = (real * spec_x[0] + imag * spec_x[1]) * factor
    across_i = (imag * spec_x[0] - real * spec_x[1]) * factor
    copies = []

    def exchange_grad(half, value):
        base, place = half * N1, pl.ds(half * 4, 4)
        c_lin[pl.ds(base, HALF, stride=2), :] = value[:, :LANES]
        c_lin[pl.ds(base + 1, HALF, stride=2), :] = value[:, LANES:]
        copies.append(swap(cbuf.at[place, pl.ds(2 * (1 - core), 2)], cgot.at[place], 9 + 7 * half))

    inverse(across_r, across_i, exchange_grad)

    for half in (0, 1):
        copies[half].wait()
        place = pl.ds(half * 4, 4)
        csum[place] = cbuf[place, pl.ds(2 * core, 2)] + cgot[place]
        for far in FAR_FIRST:
            to = (plane + far) % 8
            piece = pl.ds(pl.multiple_of((to // 2) * 8, 8), 8)
            deliver(
                csum.at[place, to % 2, piece], along_y.at[half, plane], 11 + 6 * half, 2 * to + core, at
            )

    loss_own[...] = jnp.sum(loss_acc[...], axis=0, keepdims=True)

    def send_loss(step, carry):
        deliver(loss_own, loss_mid.at[plane], 8, 2 * ((plane + step) % 8) + core, at)
        return carry

    lax.fori_loop(0, 8, send_loss, 0)

    def send_predicted(step, carry):
        to = (step + at + 14) % 32
        deliver(
            pbuf.at[to, own_half], pred_out.at[owner_row, own_half], 7, 2 * plane + owner_core, to
        )
        return carry

    lax.fori_loop(0, 32, send_predicted, 0)

    arrived(loss_mid, 8)
    loss_sum[...] = jnp.sum(loss_mid[...], axis=0)

    def send_loss_sum(step, carry):
        deliver(loss_sum, loss_all.at[at], 10, group, (at + step) % 32)
        return carry

    lax.fori_loop(0, 32, send_loss_sum, 0)

    for half in (0, 1):
        arrived(along_y.at[half], 11 + 6 * half)
        along_sum[pl.ds(half * 4, 4)] = jnp.sum(along_y[half], axis=0)
        for step in range(half * 4, half * 4 + 4):
            deliver(
                along_sum.at[step], across.at[owner_row // 2, owner_core], 12,
                2 * plane + row_odd, 4 * step + 2 * core + on_plane,
            )

    @pl.when(active)
    def _():
        arrived(across, 12)
        across_sum[...] = across[:, 0] + across[:, 1]

        for far in FAR_FIRST:
            deliver(
                across_sum, grad_out.at[:, core, own_piece], 13, 2 * ((plane + far) % 8) + core, at
            )

    arrived(loss_all, 10)
    everything = jnp.sum(jnp.sum(loss_all[...], axis=0), keepdims=True)
    loss_out[...] = everything / (CHANNELS * (LENGTH - 1))

    arrived(grad_out.at[:, core], 13)
    copy = swap(grad_out.at[:, core], grad_out.at[:, core], 14)

    def drain(less, whole, part, number):
        @pl.when(less)
        def _():
            sent(part, number)

        @pl.when(jnp.logical_not(less))
        def _():
            sent(whole, number)

    own_core = owner_core == core
    drain(own_core, xbuf.at[:, pl.ds(0, 16)], xbuf.at[pl.ds(0, 31), pl.ds(0, 16)], 0)

    @pl.when(active)
    def _():
        drain(
            jnp.logical_and(own_core, row_odd == core),
            xbuf.at[pl.ds(0, 16), pl.ds(0, 8)], xbuf.at[pl.ds(0, 15), pl.ds(0, 8)], 2,
        )
        sent(xbuf.at[pl.ds(0, 14)], 13)

    sent(xbuf.at[pl.ds(0, 14)], 3)
    drain(own_core, xbuf.at[:, pl.ds(0, 16)], xbuf.at[pl.ds(0, 31), pl.ds(0, 16)], 7)
    sent(loss_mid.at[pl.ds(0, 7)], 8)
    sent(loss_all.at[pl.ds(0, 31)], 10)
    sent(xbuf.at[pl.ds(0, 7)], 11)
    sent(xbuf.at[pl.ds(0, 7)], 17)
    drain(
        jnp.logical_and(active, row_odd == core), along_sum, along_sum.at[pl.ds(0, 7)], 12
    )
    arrived(pred_out, 7)
    copy.wait()


def per_device(signal, filters, gate_scale, gate_shift):
    (outer_h, outer_l), (outer_th, outer_tl), (inner_h, inner_l), twist, lane = make_tables()
    vmem = pl.BlockSpec(memory_space=pltpu.VMEM)
    anywhere = pl.BlockSpec(memory_space=pl.ANY)

    def space(*shape, kind=f32):
        return pltpu.VMEM(shape, kind)

    predicted, grad, loss = pl.pallas_call(
        kernel,
        out_shape=(
            pltpu.VMEM((16, SEGS, LANES), f32),
            pltpu.VMEM((8, 2, SEGS, LANES), f32),
            jax.ShapeDtypeStruct((1, 1), f32),
        ),
        in_specs=[anywhere] * 2 + [vmem] * 2 + [anywhere] * 7 + [vmem],
        out_specs=(vmem, vmem, vmem),
        scratch_shapes=[
            space(16, 4096), space(16, 1024), space(512, LANES), space(128, LANES), space(8, LANES), space(8, LANES),
            space(SHARDS, SEGS, LANES), space(8, 4, SEGS, LANES), space(SHARDS, SEGS, LANES),
            space(N1, N2), space(N1, N2), space(8, 4, SEGS, LANES), space(8, 2, SEGS, LANES),
            space(8, 2, SEGS, LANES), space(2, 8, 4, 8, LANES), space(8, 8, LANES),
            space(8, 2, 8, LANES), space(8, 8, LANES),
            space(8, LANES), space(1, LANES), space(8, 1, LANES), space(1, LANES), space(32, 1, LANES),
            space(N1, 3 * N1, kind=bf16), space(N1, 3 * N1, kind=bf16), space(3 * N2, 2 * N2, kind=bf16),
            space(2, HALF, N2),
            space(3 * N1, N2, kind=bf16), space(3 * N1, N2, kind=bf16),
            space(N2, N2, kind=bf16), space(N1, N1, kind=bf16), space(N1, N2),
            space(N1, N2), space(N1, N2), space(N1, N2), space(3 * N1, N2, kind=bf16),
            space(N1, 3 * N2, kind=bf16), space(2, HALF, N2),
            pltpu.SemaphoreType.DMA((12,)), pltpu.SemaphoreType.DMA((18,)), pltpu.SemaphoreType.DMA((18,)),
        ],
        compiler_params=pltpu.CompilerParams(has_side_effects=True, collective_id=1),
    )(
        signal, filters, gate_scale.reshape(1, 16), gate_shift.reshape(1, 16),
        outer_h, outer_l, outer_th, outer_tl, inner_h, inner_l, twist, lane,
    )
    return (predicted.reshape(16, 4096), grad.reshape(16, 4096), loss.reshape(()))


def solution(mesh):
    return jax.shard_map(
        per_device,
        mesh=mesh,
        in_specs=(P("chan", "tm"), P(None, "tm"), P("chan"), P("chan")),
        out_specs=(P("chan", "tm"), P(None, "tm"), P()),
        check_vma=False,
    )
```

```python
import math

import jax
import jax.numpy as jnp
import numpy as np
from jax import lax
from jax.experimental import pallas as pl
from jax.experimental.pallas import tpu as pltpu
from jax.sharding import PartitionSpec as P

CHANNELS = 256
LENGTH = 131072
N1, N2 = 512, 256
HALF = 256
SHARDS = 32
SEGS = 32
LANES = 128
var_floor = 1.0
MESH = pl.DeviceIdType.MESH
FAR_FIRST = (4, 3, 5, 2, 6, 1, 7, 0)
f32, bf16 = jnp.float32, jnp.bfloat16


def split_table(table):
    high = table.astype(np.float32).astype(bf16)
    low = (table - np.asarray(high).astype(np.float64)).astype(np.float32).astype(bf16)
    return np.asarray(high), np.asarray(low)


def make_tables():
    n1, n2 = np.arange(N1), np.arange(N2)
    k1 = np.arange(HALF)
    angle = 2 * math.pi * ((np.outer(4 * k1 + 1, n1) % (4 * N1)) / (4 * N1))
    outer = np.concatenate([np.cos(angle), -np.sin(angle)], axis=0)
    angle = 2 * math.pi * ((np.outer(n2, n2) % N2) / N2)
    inner = np.concatenate([np.cos(angle), np.sin(angle)], axis=1)
    angle = 2 * math.pi * (np.outer(4 * k1 + 1, n2) / (4 * LENGTH))
    twist = np.stack([np.cos(angle), -np.sin(angle)]).astype(np.float32)
    angle = math.pi * n2 / 256
    lane = np.zeros((8, N2), np.float32)
    lane[0], lane[1] = np.cos(angle), -np.sin(angle)
    return split_table(outer), split_table(outer.T), split_table(inner), twist, lane


def high_low(value):
    high = value.astype(bf16)
    return high, (value - high.astype(f32)).astype(bf16)


def three_way(value):
    high = value.astype(bf16)
    rest = value - high.astype(f32)
    middle = rest.astype(bf16)
    return high, middle, (rest - middle.astype(f32)).astype(bf16)


def dot(first, second):
    return jnp.dot(first, second, preferred_element_type=f32)


def kernel(
    signal_hbm, filters_hbm, scale_in, shift_in,
    outer_h, outer_l, outer_th, outer_tl, inner_h, inner_l, twist_hbm, lane_ref,
    pred_out, grad_out, loss_out,
    signal, filters, signal_send, filter_send, gate_send, gate_got,
    xbuf, fbuf, pbuf, ybuf, ygot, cbuf, cgot, csum, along_y, along_sum, across, across_sum,
    loss_acc, loss_own, loss_mid, loss_sum, loss_all,
    outer_k, outer_tk, inner_k, twist,
    triple_x, triple_q, tri_up, tri_low, totals,
    spread_s, normed_s, gating_s, stack, left, spec_x,
    table_sem, send_sem, recv_sem,
):
    group, at = lax.axis_index("chan"), lax.axis_index("tm")
    plane, core = group // 2, group % 2
    owner_core, owner_row = at % 2, at // 2
    depth, width = at // 4, at % 4
    partner = 2 * plane + 1 - core
    own_half = pl.ds(pl.multiple_of(core * 16, 16), 16)
    own_piece = pl.ds(pl.multiple_of((plane // 2) * 8, 8), 8)
    on_plane = plane % 2
    active = at % 2 == on_plane
    row_odd = owner_row % 2

    barrier = pltpu.get_barrier_semaphore()

    def greet(chan, tm):
        pl.semaphore_signal(barrier, inc=1, device_id=(chan, tm), device_id_type=MESH)

    for far in FAR_FIRST[:-1]:
        for step in range(8):
            greet(2 * plane + step % 2, 4 * ((depth + far) % 8) + step // 2)
    for far in FAR_FIRST[:-1]:
        greet(2 * ((plane + far) % 8) + core, at)
    for side in (2, 1, 3):
        for step in (0, 1):
            greet(2 * plane + step, 4 * depth + (width + side) % 4)
    greet(partner, at)

    def fetch(source, target, number):
        return pltpu.make_async_copy(source, target, table_sem.at[number])

    tables = [
        (outer_h, outer_k.at[:, pl.ds(0, N1)]), (outer_h, outer_k.at[:, pl.ds(N1, N1)]),
        (outer_l, outer_k.at[:, pl.ds(2 * N1, N1)]),
        (outer_th, outer_tk.at[:, pl.ds(0, N1)]), (outer_th, outer_tk.at[:, pl.ds(N1, N1)]),
        (outer_tl, outer_tk.at[:, pl.ds(2 * N1, N1)]),
        (inner_h, inner_k.at[pl.ds(0, N2)]), (inner_h, inner_k.at[pl.ds(N2, N2)]),
        (inner_l, inner_k.at[pl.ds(2 * N2, N2)]),
        (twist_hbm, twist),
    ]
    own_taps = pl.ds(pl.multiple_of((plane // 2) * 1024, 1024), 1024)
    inputs = [(signal_hbm, signal), (filters_hbm.at[:, own_taps], filters)]
    for number, (source, target) in enumerate(inputs):
        fetch(source, target, 10 + number).start()
    for number, (source, target) in enumerate(tables):
        fetch(source, target, number).start()

    def remote(source, target, number, chan, tm):
        return pltpu.make_async_remote_copy(
            src_ref=source, dst_ref=target, send_sem=send_sem.at[number], recv_sem=recv_sem.at[number],
            device_id=(chan, tm), device_id_type=MESH,
        )

    def deliver(source, target, number, chan, tm):
        here = jnp.logical_and(chan == group, tm == at)

        @pl.when(jnp.logical_not(here))
        def _():
            remote(source, target, number, chan, tm).start()

        @pl.when(here)
        def _():
            pltpu.make_async_copy(source, target, recv_sem.at[number]).start()

    def deliver_far(far, source, target, number, chan, tm):
        if far:
            remote(source, target, number, chan, tm).start()
        else:
            deliver(source, target, number, chan, tm)

    def arrived(target, number):
        pltpu.make_async_copy(target, target, recv_sem.at[number]).wait()

    def sent(source, number):
        pltpu.make_async_copy(source, source, send_sem.at[number]).wait()

    def swap(source, target, number):
        copy = remote(source, target, number, partner, at)
        copy.start()
        return copy

    def signal_turn(seg, carry):
        signal_send[pl.ds(seg, 16, stride=SEGS), :] = signal[:, pl.ds(pl.multiple_of(seg * LANES, LANES), LANES)]
        return carry

    fetch(*inputs[0], 10).wait()
    lax.fori_loop(0, SEGS, signal_turn, 0, unroll=4)
    signal_rows = signal_send.reshape(16, SEGS, LANES)
    gate_send[...] = jnp.zeros((8, LANES), f32)
    gate_send[0:1, 0:16] = scale_in[...]
    gate_send[1:2, 0:16] = shift_in[...]
    fetch(*inputs[1], 11).wait()
    for seg in range(8):
        filter_send[pl.ds(seg, 16, stride=8), :] = filters[:, seg * LANES : (seg + 1) * LANES]
    filter_rows = filter_send.reshape(16, 8, LANES)

    pl.semaphore_wait(barrier, 2 * SHARDS - 1 + 7)

    @pl.when(active)
    def _():
        for far in FAR_FIRST:
            for side in (0, 1):
                row = 2 * ((depth + far) % 8) + side
                deliver_far(
                    far, filter_rows.at[row], fbuf.at[depth, width, own_piece], 2,
                    2 * plane + row_odd, 2 * row + core,
                )

    for far in FAR_FIRST:
        for side in (0, 1):
            row = 2 * ((depth + far) % 8) + side
            for half in (0, 1):
                part = pl.ds(half * 16, 16)
                deliver_far(
                    far, signal_rows.at[row, part], xbuf.at[at, part], 0, 2 * plane + half, 2 * row + core
                )
    gates = swap(gate_send, gate_got, 1)

    row_up = lax.broadcasted_iota(jnp.int32, (N2, N2), 0)
    col_up = lax.broadcasted_iota(jnp.int32, (N2, N2), 1)
    tri_up[...] = jnp.where(row_up <= col_up, 1.0, 0.0).astype(bf16)

    def rows(q, offset=0):
        return pl.ds(pl.multiple_of(q * 32 + offset, 32), 32)

    row_low = lax.broadcasted_iota(jnp.int32, (32, N1), 0)
    col_low = lax.broadcasted_iota(jnp.int32, (32, N1), 1)

    def fill_low(q, carry):
        tri_low[rows(q), :] = jnp.where(col_low < row_low + q * 32, 1.0, 0.0).astype(bf16)
        return carry

    lax.fori_loop(0, 16, fill_low, 0)

    for number, (source, target) in enumerate(tables):
        fetch(source, target, number).wait()
    core_f = core.astype(f32)
    lane_r = 1.0 + core_f * (lane_ref[0:1, :] - 1.0)
    lane_i = core_f * lane_ref[1:2, :]
    base_r, base_i = twist[0], twist[1]
    twist[0] = base_r * lane_r - base_i * lane_i
    twist[1] = base_r * lane_i + base_i * lane_r

    rows_here = lax.broadcasted_iota(jnp.int32, (32, 1), 0)
    flip = 1.0 - 2.0 * core_f * (rows_here % 2).astype(f32)
    half_rows = lax.broadcasted_iota(jnp.int32, (HALF, 1), 0)
    flip_half = 1.0 - 2.0 * core_f * (half_rows % 2).astype(f32)

    x_lin = xbuf.reshape(SHARDS * SEGS, LANES)
    f_lin = fbuf.reshape(SHARDS * SEGS, LANES)
    p_lin = pbuf.reshape(SHARDS * SEGS, LANES)
    c_lin = cbuf.reshape(SHARDS * SEGS, LANES)

    def pair_rows(ref, q):
        base = pl.multiple_of(q * 64, 64)
        return jnp.concatenate(
            [ref[pl.ds(base, 32, stride=2), :], ref[pl.ds(base + 1, 32, stride=2), :]], axis=1
        )

    def put_pairs(ref, q, value):
        base = pl.multiple_of(q * 64, 64)
        ref[pl.ds(base, 32, stride=2), :] = value[:, :LANES]
        ref[pl.ds(base + 1, 32, stride=2), :] = value[:, LANES:]

    def fill_stack(q, value):
        high, low = high_low(value * flip)
        stack[rows(q), :] = high
        stack[rows(q, N1), :] = low
        stack[rows(q, 2 * N1), :] = high

    def fill_left(real, imag):
        for part, value in enumerate((real, imag)):
            high, low = high_low(value)
            place = slice(part * HALF, (part + 1) * HALF)
            left[place, 0:N2] = high
            left[place, N2 : 2 * N2] = low
            left[place, 2 * N2 : 3 * N2] = high

    def forward():
        first = dot(outer_k[...], stack[...])
        first_r, first_i = first[:HALF], first[HALF:]
        fill_left(first_r * twist[0] - first_i * twist[1], first_r * twist[1] + first_i * twist[0])
        quads = dot(left[...], inner_k[...])
        return quads[:HALF, :N2] + quads[HALF:, N2:], quads[HALF:, :N2] - quads[:HALF, N2:]

    def inverse(real, imag, take):
        fill_left(real, imag)
        quads = dot(left[...], inner_k[...])
        mid_r = quads[:HALF, :N2] - quads[HALF:, N2:]
        mid_i = quads[HALF:, :N2] + quads[:HALF, N2:]
        high, low = high_low(mid_r * twist[0] + mid_i * twist[1])
        stack[0:HALF, :] = high
        stack[N1 : N1 + HALF, :] = low
        stack[2 * N1 : 2 * N1 + HALF, :] = high
        high, low = high_low(mid_i * twist[0] - mid_r * twist[1])
        stack[HALF:N1, :] = high
        stack[N1 + HALF : 2 * N1, :] = low
        stack[2 * N1 + HALF : 3 * N1, :] = high
        for half in (0, 1):
            place = slice(half * HALF, (half + 1) * HALF)
            take(half, dot(outer_tk[place, :], stack[...]) * flip_half)

    own_blocks = fbuf.at[:, 2 * core + on_plane, own_piece]
    arrived(own_blocks, 2)

    for far in FAR_FIRST[:-1]:
        remote(own_blocks, own_blocks, 3, 2 * ((plane + far) % 8) + core, at).start()
    arrived(xbuf.at[:, own_half], 0)
    copy = swap(xbuf.at[:, own_half], xbuf.at[:, own_half], 4)
    copy.wait()

    def split_rows(q, carry):
        value = pair_rows(x_lin, q)
        for part, piece in enumerate(three_way(value)):
            triple_x[rows(q, part * N1), :] = piece
        for part, piece in enumerate(three_way(value * value)):
            triple_q[rows(q, part * N1), :] = piece
        return carry

    lax.fori_loop(0, 16, split_rows, 0, unroll=2)
    sums = dot(triple_x[...], tri_up[...])
    normed_s[...] = sums[:N1] + sums[N1 : 2 * N1] + sums[2 * N1 :]
    sums = dot(triple_q[...], tri_up[...])
    spread_s[...] = sums[:N1] + sums[N1 : 2 * N1] + sums[2 * N1 :]
    row_sums = jnp.concatenate(
        [
            jnp.broadcast_to(normed_s[:, N2 - 1 : N2], (N1, LANES)),
            jnp.broadcast_to(spread_s[:, N2 - 1 : N2], (N1, LANES)),
        ],
        axis=1,
    )
    carried = dot(tri_low[...], jnp.concatenate(three_way(row_sums), axis=1))
    totals[...] = carried[:, :N2] + carried[:, N2 : 2 * N2] + carried[:, 2 * N2 :]

    gates.wait()
    gate_pair = jnp.where(core == owner_core, gate_send[...], gate_got[...])
    pick = lax.broadcasted_iota(jnp.int32, (1, LANES), 1) == owner_row
    gate_gain = jnp.sum(jnp.where(pick, gate_pair[0:1, :], 0.0), axis=1, keepdims=True)
    gate_bias = jnp.sum(jnp.where(pick, gate_pair[1:2, :], 0.0), axis=1, keepdims=True)

    lane_index = lax.broadcasted_iota(jnp.int32, (32, N2), 1)
    row_index = lax.broadcasted_iota(jnp.int32, (32, N2), 0)

    def normalize(q, carry):
        value = pair_rows(x_lin, q)
        before = totals[rows(q), :]
        first = normed_s[rows(q), :] + jnp.concatenate([before[:, :LANES]] * 2, axis=1)
        second = spread_s[rows(q), :] + jnp.concatenate([before[:, LANES:]] * 2, axis=1)
        counts = ((q * 32 + row_index) * N2 + lane_index + 1).astype(f32)
        mean = first / counts
        variance = second / counts - mean * mean
        spread = jnp.sqrt(jnp.maximum(variance, var_floor))
        normed = (value - mean) / spread
        gating_s[rows(q), :] = 1.0 / (1.0 + jnp.exp(-(gate_gain * normed + gate_bias)))
        spread_s[rows(q), :] = spread
        fill_stack(q, normed)
        return carry

    lax.fori_loop(0, 16, normalize, 0, unroll=2)
    arrived(xbuf.at[pl.ds(0, 14)], 3)
    core_blocks = fbuf.at[:, pl.ds(2 * core, 2)]
    copy = swap(core_blocks, core_blocks, 5)
    real, imag = forward()
    spec_x[0], spec_x[1] = real, imag
    copy.wait()

    def take_filter(q, carry):
        fill_stack(q, pair_rows(f_lin, q))
        return carry

    lax.fori_loop(0, 16, take_filter, 0, unroll=2)
    real, imag = forward()
    factor = 1.0 / math.sqrt(LENGTH) / LENGTH
    real, imag = real * factor, imag * factor
    copies = []

    def exchange(half, value):
        place = pl.ds(half * HALF, HALF)
        ybuf[place, :] = value
        copies.append(swap(ybuf.at[place], ygot.at[place], 6 + 9 * half))

    inverse(
        spec_x[0] * real - spec_x[1] * imag, spec_x[0] * imag + spec_x[1] * real, exchange
    )

    loss_acc[...] = jnp.zeros((8, LANES), f32)

    def predict(q, carry):
        value = pair_rows(x_lin, q)
        opening = x_lin[pl.ds(pl.multiple_of(q * 64, 64), 32, stride=2), :][:, 0:1]
        after = jnp.minimum(q * 64 + 64, SHARDS * SEGS - 8)
        following = x_lin[pl.ds(pl.multiple_of(after, 8), 8), :][0:1, 0:1]
        edge = jnp.concatenate([opening[1:], following], axis=0)
        target = jnp.concatenate([value[:, 1:], edge], axis=1)
        weight = spread_s[rows(q), :] * gating_s[rows(q), :]
        predicted = value + weight * (ybuf[rows(q), :] + ygot[rows(q), :])
        put_pairs(p_lin, q, predicted)
        step_index = (q * 32 + row_index) * N2 + lane_index
        residual = jnp.where(step_index < LENGTH - 1, predicted - target, 0.0)
        squares = residual * residual
        squares = squares[:, :LANES] + squares[:, LANES:]
        loss_acc[...] += (squares[0:8] + squares[8:16]) + (squares[16:24] + squares[24:32])
        fill_stack(q, (2.0 / CHANNELS) * residual * weight)
        return carry

    copies[0].wait()
    lax.fori_loop(0, 8, predict, 0, unroll=2)
    copies[1].wait()
    lax.fori_loop(8, 16, predict, 0, unroll=2)

    loss_own[...] = jnp.sum(loss_acc[...], axis=0, keepdims=True)

    def send_loss(step, carry):
        deliver(loss_own, loss_mid.at[plane], 8, 2 * ((plane + step) % 8) + core, at)
        return carry

    lax.fori_loop(0, 8, send_loss, 0)

    for far in FAR_FIRST:
        for side in (2, 1, 3, 0):
            to = 4 * ((depth + far) % 8) + (width + side) % 4
            deliver_far(
                far + side, pbuf.at[to, own_half], pred_out.at[owner_row, own_half], 7,
                2 * plane + owner_core, to,
            )

    real, imag = forward()
    across_r = (real * spec_x[0] + imag * spec_x[1]) * factor
    across_i = (imag * spec_x[0] - real * spec_x[1]) * factor
    copies = []

    def exchange_grad(half, value):
        base, place = half * N1, pl.ds(half * 4, 4)
        c_lin[pl.ds(base, HALF, stride=2), :] = value[:, :LANES]
        c_lin[pl.ds(base + 1, HALF, stride=2), :] = value[:, LANES:]
        copies.append(swap(cbuf.at[place, pl.ds(2 * (1 - core), 2)], cgot.at[place], 9 + 7 * half))

    inverse(across_r, across_i, exchange_grad)

    for half in (0, 1):
        copies[half].wait()
        place = pl.ds(half * 4, 4)
        csum[place] = cbuf[place, pl.ds(2 * core, 2)] + cgot[place]
        for far in FAR_FIRST:
            to = (plane + far) % 8
            piece = pl.ds(pl.multiple_of((to // 2) * 8, 8), 8)
            deliver_far(
                far, csum.at[place, to % 2, piece], along_y.at[half, plane], 11 + 6 * half, 2 * to + core, at
            )

    arrived(loss_mid, 8)
    loss_sum[...] = jnp.sum(loss_mid[...], axis=0)

    def send_loss_sum(step, carry):
        deliver(loss_sum, loss_all.at[at], 10, group, (at + step) % 32)
        return carry

    lax.fori_loop(0, 32, send_loss_sum, 0)

    for half in (0, 1):
        arrived(along_y.at[half], 11 + 6 * half)
        along_sum[pl.ds(half * 4, 4)] = jnp.sum(along_y[half], axis=0)
        for step in range(half * 4, half * 4 + 4):
            deliver(
                along_sum.at[step], across.at[owner_row // 2, owner_core], 12,
                2 * plane + row_odd, 4 * step + 2 * core + on_plane,
            )

    @pl.when(active)
    def _():
        arrived(across, 12)
        across_sum[...] = across[:, 0] + across[:, 1]

        for far in FAR_FIRST:
            deliver_far(
                far, across_sum, grad_out.at[:, core, own_piece], 13, 2 * ((plane + far) % 8) + core, at
            )

    arrived(loss_all, 10)
    everything = jnp.sum(jnp.sum(loss_all[...], axis=0), keepdims=True)
    loss_out[...] = everything / (CHANNELS * (LENGTH - 1))

    arrived(grad_out.at[:, core], 13)
    copy = swap(grad_out.at[:, core], grad_out.at[:, core], 14)

    def drain(less, whole, part, number):
        @pl.when(less)
        def _():
            sent(part, number)

        @pl.when(jnp.logical_not(less))
        def _():
            sent(whole, number)

    own_core = owner_core == core
    drain(own_core, xbuf.at[:, pl.ds(0, 16)], xbuf.at[pl.ds(0, 31), pl.ds(0, 16)], 0)

    @pl.when(active)
    def _():
        drain(
            jnp.logical_and(own_core, row_odd == core),
            xbuf.at[pl.ds(0, 16), pl.ds(0, 8)], xbuf.at[pl.ds(0, 15), pl.ds(0, 8)], 2,
        )
        sent(xbuf.at[pl.ds(0, 14)], 13)

    sent(xbuf.at[pl.ds(0, 14)], 3)
    drain(own_core, xbuf.at[:, pl.ds(0, 16)], xbuf.at[pl.ds(0, 31), pl.ds(0, 16)], 7)
    sent(loss_mid.at[pl.ds(0, 7)], 8)
    sent(loss_all.at[pl.ds(0, 31)], 10)
    sent(xbuf.at[pl.ds(0, 7)], 11)
    sent(xbuf.at[pl.ds(0, 7)], 17)
    drain(
        jnp.logical_and(active, row_odd == core), along_sum, along_sum.at[pl.ds(0, 7)], 12
    )
    arrived(pred_out, 7)
    copy.wait()


def per_device(signal, filters, gate_scale, gate_shift):
    (outer_h, outer_l), (outer_th, outer_tl), (inner_h, inner_l), twist, lane = make_tables()
    vmem = pl.BlockSpec(memory_space=pltpu.VMEM)
    anywhere = pl.BlockSpec(memory_space=pl.ANY)

    def space(*shape, kind=f32):
        return pltpu.VMEM(shape, kind)

    predicted, grad, loss = pl.pallas_call(
        kernel,
        out_shape=(
            pltpu.VMEM((16, SEGS, LANES), f32),
            pltpu.VMEM((8, 2, SEGS, LANES), f32),
            jax.ShapeDtypeStruct((1, 1), f32),
        ),
        in_specs=[anywhere] * 2 + [vmem] * 2 + [anywhere] * 7 + [vmem],
        out_specs=(vmem, vmem, vmem),
        scratch_shapes=[
            space(16, 4096), space(16, 1024), space(512, LANES), space(128, LANES), space(8, LANES), space(8, LANES),
            space(SHARDS, SEGS, LANES), space(8, 4, SEGS, LANES), space(SHARDS, SEGS, LANES),
            space(N1, N2), space(N1, N2), space(8, 4, SEGS, LANES), space(8, 2, SEGS, LANES),
            space(8, 2, SEGS, LANES), space(2, 8, 4, 8, LANES), space(8, 8, LANES),
            space(8, 2, 8, LANES), space(8, 8, LANES),
            space(8, LANES), space(1, LANES), space(8, 1, LANES), space(1, LANES), space(32, 1, LANES),
            space(N1, 3 * N1, kind=bf16), space(N1, 3 * N1, kind=bf16), space(3 * N2, 2 * N2, kind=bf16),
            space(2, HALF, N2),
            space(3 * N1, N2, kind=bf16), space(3 * N1, N2, kind=bf16),
            space(N2, N2, kind=bf16), space(N1, N1, kind=bf16), space(N1, N2),
            space(N1, N2), space(N1, N2), space(N1, N2), space(3 * N1, N2, kind=bf16),
            space(N1, 3 * N2, kind=bf16), space(2, HALF, N2),
            pltpu.SemaphoreType.DMA((12,)), pltpu.SemaphoreType.DMA((18,)), pltpu.SemaphoreType.DMA((18,)),
        ],
        compiler_params=pltpu.CompilerParams(has_side_effects=True, collective_id=1),
    )(
        signal, filters, gate_scale.reshape(1, 16), gate_shift.reshape(1, 16),
        outer_h, outer_l, outer_th, outer_tl, inner_h, inner_l, twist, lane,
    )
    return (predicted.reshape(16, 4096), grad.reshape(16, 4096), loss.reshape(()))


def solution(mesh):
    return jax.shard_map(
        per_device,
        mesh=mesh,
        in_specs=(P("chan", "tm"), P(None, "tm"), P("chan"), P("chan")),
        out_specs=(P("chan", "tm"), P(None, "tm"), P()),
        check_vma=False,
    )
```

```python
import math

import jax
import jax.numpy as jnp
import numpy as np
from jax import lax
from jax.experimental import pallas as pl
from jax.experimental.pallas import tpu as pltpu
from jax.sharding import PartitionSpec as P

CHANNELS = 256
LENGTH = 131072
N1, N2 = 512, 256
HALF = 256
SHARDS = 32
SEGS = 32
LANES = 128
var_floor = 1.0
MESH = pl.DeviceIdType.MESH
FAR_FIRST = (4, 3, 5, 2, 6, 1, 7, 0)
f32, bf16 = jnp.float32, jnp.bfloat16


def split_table(table):
    high = table.astype(np.float32).astype(bf16)
    low = (table - np.asarray(high).astype(np.float64)).astype(np.float32).astype(bf16)
    return np.asarray(high), np.asarray(low)


def make_tables():
    n1, n2 = np.arange(N1), np.arange(N2)
    k1 = np.arange(HALF)
    angle = 2 * math.pi * ((np.outer(4 * k1 + 1, n1) % (4 * N1)) / (4 * N1))
    outer = np.concatenate([np.cos(angle), -np.sin(angle)], axis=0)
    angle = 2 * math.pi * ((np.outer(n2, n2) % N2) / N2)
    inner = np.concatenate([np.cos(angle), np.sin(angle)], axis=1)
    angle = 2 * math.pi * (np.outer(4 * k1 + 1, n2) / (4 * LENGTH))
    twist = np.stack([np.cos(angle), -np.sin(angle)]).astype(np.float32)
    angle = math.pi * n2 / 256
    lane = np.zeros((8, N2), np.float32)
    lane[0], lane[1] = np.cos(angle), -np.sin(angle)
    return split_table(outer), split_table(outer.T), split_table(inner), twist, lane


def high_low(value):
    high = value.astype(bf16)
    return high, (value - high.astype(f32)).astype(bf16)


def three_way(value):
    high = value.astype(bf16)
    rest = value - high.astype(f32)
    middle = rest.astype(bf16)
    return high, middle, (rest - middle.astype(f32)).astype(bf16)


def dot(first, second):
    return jnp.dot(first, second, preferred_element_type=f32)


def kernel(
    signal_hbm, filters_hbm, scale_hbm, shift_hbm,
    outer_h, outer_l, outer_th, outer_tl, inner_h, inner_l, twist_hbm, lane_hbm,
    pred_out, grad_out, loss_out,
    signal, filters, scale_in, shift_in, lane_ref, signal_send, filter_send, gate_send, gate_got,
    xbuf, fbuf, pbuf, ybuf, ygot, cbuf, cgot, csum, along_y, along_sum, across, across_sum,
    loss_acc, loss_own, loss_mid, loss_sum, loss_all,
    outer_k, outer_tk, inner_k, twist,
    triple_x, triple_q, tri_up, tri_low, totals,
    spread_s, normed_s, gating_s, stack, left, spec_x,
    table_sem, send_sem, recv_sem,
):
    group, at = lax.axis_index("chan"), lax.axis_index("tm")
    plane, core = group // 2, group % 2
    owner_core, owner_row = at % 2, at // 2
    depth, width = at // 4, at % 4
    partner = 2 * plane + 1 - core
    own_half = pl.ds(pl.multiple_of(core * 16, 16), 16)
    own_piece = pl.ds(pl.multiple_of((plane // 2) * 8, 8), 8)
    on_plane = plane % 2
    active = at % 2 == on_plane
    row_odd = owner_row % 2

    barrier = pltpu.get_barrier_semaphore()

    def greet(chan, tm):
        pl.semaphore_signal(barrier, inc=1, device_id=(chan, tm), device_id_type=MESH)

    for far in FAR_FIRST[:-1]:
        for step in range(8):
            greet(2 * plane + step % 2, 4 * ((depth + far) % 8) + step // 2)
    for far in FAR_FIRST[:-1]:
        greet(2 * ((plane + far) % 8) + core, at)
    for side in (2, 1, 3):
        for step in (0, 1):
            greet(2 * plane + step, 4 * depth + (width + side) % 4)
    greet(partner, at)

    def fetch(source, target, number):
        return pltpu.make_async_copy(source, target, table_sem.at[number])

    tables = [
        (outer_h, outer_k.at[:, pl.ds(0, N1)]), (outer_h, outer_k.at[:, pl.ds(N1, N1)]),
        (outer_l, outer_k.at[:, pl.ds(2 * N1, N1)]),
        (outer_th, outer_tk.at[:, pl.ds(0, N1)]), (outer_th, outer_tk.at[:, pl.ds(N1, N1)]),
        (outer_tl, outer_tk.at[:, pl.ds(2 * N1, N1)]),
        (inner_h, inner_k.at[pl.ds(0, N2)]), (inner_h, inner_k.at[pl.ds(N2, N2)]),
        (inner_l, inner_k.at[pl.ds(2 * N2, N2)]),
        (twist_hbm, twist), (lane_hbm, lane_ref), (scale_hbm, scale_in), (shift_hbm, shift_in),
    ]
    own_taps = pl.ds(pl.multiple_of((plane // 2) * 1024, 1024), 1024)
    inputs = [(signal_hbm, signal), (filters_hbm.at[:, own_taps], filters)]
    for number, (source, target) in enumerate(inputs):
        fetch(source, target, 13 + number).start()
    for number, (source, target) in enumerate(tables):
        fetch(source, target, number).start()

    def remote(source, target, number, chan, tm):
        return pltpu.make_async_remote_copy(
            src_ref=source, dst_ref=target, send_sem=send_sem.at[number], recv_sem=recv_sem.at[number],
            device_id=(chan, tm), device_id_type=MESH,
        )

    def deliver(source, target, number, chan, tm):
        here = jnp.logical_and(chan == group, tm == at)

        @pl.when(jnp.logical_not(here))
        def _():
            remote(source, target, number, chan, tm).start()

        @pl.when(here)
        def _():
            pltpu.make_async_copy(source, target, recv_sem.at[number]).start()

    def deliver_far(far, source, target, number, chan, tm):
        if far:
            remote(source, target, number, chan, tm).start()
        else:
            deliver(source, target, number, chan, tm)

    def arrived(target, number):
        pltpu.make_async_copy(target, target, recv_sem.at[number]).wait()

    def sent(source, number):
        pltpu.make_async_copy(source, source, send_sem.at[number]).wait()

    def swap(source, target, number):
        copy = remote(source, target, number, partner, at)
        copy.start()
        return copy

    def signal_turn(seg, carry):
        signal_send[pl.ds(seg, 16, stride=SEGS), :] = signal[:, pl.ds(pl.multiple_of(seg * LANES, LANES), LANES)]
        return carry

    fetch(*inputs[0], 13).wait()
    lax.fori_loop(0, SEGS, signal_turn, 0, unroll=4)
    signal_rows = signal_send.reshape(16, SEGS, LANES)
    fetch(*inputs[1], 14).wait()
    for seg in range(8):
        filter_send[pl.ds(seg, 16, stride=8), :] = filters[:, seg * LANES : (seg + 1) * LANES]
    filter_rows = filter_send.reshape(16, 8, LANES)

    pl.semaphore_wait(barrier, 2 * SHARDS - 1 + 7)

    @pl.when(active)
    def _():
        for far in FAR_FIRST:
            for side in (0, 1):
                row = 2 * ((depth + far) % 8) + side
                deliver_far(
                    far, filter_rows.at[row], fbuf.at[depth, width, own_piece], 2,
                    2 * plane + row_odd, 2 * row + core,
                )

    for far in FAR_FIRST:
        for side in (0, 1):
            row = 2 * ((depth + far) % 8) + side
            for half in (0, 1):
                part = pl.ds(half * 16, 16)
                deliver_far(
                    far, signal_rows.at[row, part], xbuf.at[at, part], 0, 2 * plane + half, 2 * row + core
                )
    row_up = lax.broadcasted_iota(jnp.int32, (N2, N2), 0)
    col_up = lax.broadcasted_iota(jnp.int32, (N2, N2), 1)
    tri_up[...] = jnp.where(row_up <= col_up, 1.0, 0.0).astype(bf16)

    def rows(q, offset=0):
        return pl.ds(pl.multiple_of(q * 32 + offset, 32), 32)

    row_low = lax.broadcasted_iota(jnp.int32, (32, N1), 0)
    col_low = lax.broadcasted_iota(jnp.int32, (32, N1), 1)

    def fill_low(q, carry):
        tri_low[rows(q), :] = jnp.where(col_low < row_low + q * 32, 1.0, 0.0).astype(bf16)
        return carry

    lax.fori_loop(0, 16, fill_low, 0)

    for number, (source, target) in enumerate(tables):
        fetch(source, target, number).wait()
    gate_send[...] = jnp.zeros((8, LANES), f32)
    gate_send[0:1, 0:16] = scale_in[...]
    gate_send[1:2, 0:16] = shift_in[...]
    gates = swap(gate_send, gate_got, 1)
    core_f = core.astype(f32)
    lane_r = 1.0 + core_f * (lane_ref[0:1, :] - 1.0)
    lane_i = core_f * lane_ref[1:2, :]
    base_r, base_i = twist[0], twist[1]
    twist[0] = base_r * lane_r - base_i * lane_i
    twist[1] = base_r * lane_i + base_i * lane_r

    rows_here = lax.broadcasted_iota(jnp.int32, (32, 1), 0)
    flip = 1.0 - 2.0 * core_f * (rows_here % 2).astype(f32)
    half_rows = lax.broadcasted_iota(jnp.int32, (HALF, 1), 0)
    flip_half = 1.0 - 2.0 * core_f * (half_rows % 2).astype(f32)

    x_lin = xbuf.reshape(SHARDS * SEGS, LANES)
    f_lin = fbuf.reshape(SHARDS * SEGS, LANES)
    p_lin = pbuf.reshape(SHARDS * SEGS, LANES)
    c_lin = cbuf.reshape(SHARDS * SEGS, LANES)

    def pair_rows(ref, q):
        base = pl.multiple_of(q * 64, 64)
        return jnp.concatenate(
            [ref[pl.ds(base, 32, stride=2), :], ref[pl.ds(base + 1, 32, stride=2), :]], axis=1
        )

    def put_pairs(ref, q, value):
        base = pl.multiple_of(q * 64, 64)
        ref[pl.ds(base, 32, stride=2), :] = value[:, :LANES]
        ref[pl.ds(base + 1, 32, stride=2), :] = value[:, LANES:]

    def fill_stack(q, value):
        high, low = high_low(value * flip)
        stack[rows(q), :] = high
        stack[rows(q, N1), :] = low
        stack[rows(q, 2 * N1), :] = high

    def fill_left(real, imag):
        for part, value in enumerate((real, imag)):
            high, low = high_low(value)
            place = slice(part * HALF, (part + 1) * HALF)
            left[place, 0:N2] = high
            left[place, N2 : 2 * N2] = low
            left[place, 2 * N2 : 3 * N2] = high

    def forward():
        first = dot(outer_k[...], stack[...])
        first_r, first_i = first[:HALF], first[HALF:]
        fill_left(first_r * twist[0] - first_i * twist[1], first_r * twist[1] + first_i * twist[0])
        quads = dot(left[...], inner_k[...])
        return quads[:HALF, :N2] + quads[HALF:, N2:], quads[HALF:, :N2] - quads[:HALF, N2:]

    def inverse(real, imag, take):
        fill_left(real, imag)
        quads = dot(left[...], inner_k[...])
        mid_r = quads[:HALF, :N2] - quads[HALF:, N2:]
        mid_i = quads[HALF:, :N2] + quads[:HALF, N2:]
        high, low = high_low(mid_r * twist[0] + mid_i * twist[1])
        stack[0:HALF, :] = high
        stack[N1 : N1 + HALF, :] = low
        stack[2 * N1 : 2 * N1 + HALF, :] = high
        high, low = high_low(mid_i * twist[0] - mid_r * twist[1])
        stack[HALF:N1, :] = high
        stack[N1 + HALF : 2 * N1, :] = low
        stack[2 * N1 + HALF : 3 * N1, :] = high
        for half in (0, 1):
            place = slice(half * HALF, (half + 1) * HALF)
            take(half, dot(outer_tk[place, :], stack[...]) * flip_half)

    own_blocks = fbuf.at[:, 2 * core + on_plane, own_piece]
    arrived(own_blocks, 2)

    for far in FAR_FIRST[:-1]:
        remote(own_blocks, own_blocks, 3, 2 * ((plane + far) % 8) + core, at).start()
    arrived(xbuf.at[:, own_half], 0)
    copy = swap(xbuf.at[:, own_half], xbuf.at[:, own_half], 4)
    copy.wait()

    def split_rows(q, carry):
        value = pair_rows(x_lin, q)
        for part, piece in enumerate(three_way(value)):
            triple_x[rows(q, part * N1), :] = piece
        for part, piece in enumerate(three_way(value * value)):
            triple_q[rows(q, part * N1), :] = piece
        return carry

    lax.fori_loop(0, 16, split_rows, 0, unroll=2)
    sums = dot(triple_x[...], tri_up[...])
    normed_s[...] = sums[:N1] + sums[N1 : 2 * N1] + sums[2 * N1 :]
    sums = dot(triple_q[...], tri_up[...])
    spread_s[...] = sums[:N1] + sums[N1 : 2 * N1] + sums[2 * N1 :]
    row_sums = jnp.concatenate(
        [
            jnp.broadcast_to(normed_s[:, N2 - 1 : N2], (N1, LANES)),
            jnp.broadcast_to(spread_s[:, N2 - 1 : N2], (N1, LANES)),
        ],
        axis=1,
    )
    carried = dot(tri_low[...], jnp.concatenate(three_way(row_sums), axis=1))
    totals[...] = carried[:, :N2] + carried[:, N2 : 2 * N2] + carried[:, 2 * N2 :]

    gates.wait()
    gate_pair = jnp.where(core == owner_core, gate_send[...], gate_got[...])
    pick = lax.broadcasted_iota(jnp.int32, (1, LANES), 1) == owner_row
    gate_gain = jnp.sum(jnp.where(pick, gate_pair[0:1, :], 0.0), axis=1, keepdims=True)
    gate_bias = jnp.sum(jnp.where(pick, gate_pair[1:2, :], 0.0), axis=1, keepdims=True)

    lane_index = lax.broadcasted_iota(jnp.int32, (32, N2), 1)
    row_index = lax.broadcasted_iota(jnp.int32, (32, N2), 0)

    def normalize(q, carry):
        value = pair_rows(x_lin, q)
        before = totals[rows(q), :]
        first = normed_s[rows(q), :] + jnp.concatenate([before[:, :LANES]] * 2, axis=1)
        second = spread_s[rows(q), :] + jnp.concatenate([before[:, LANES:]] * 2, axis=1)
        counts = ((q * 32 + row_index) * N2 + lane_index + 1).astype(f32)
        mean = first / counts
        variance = second / counts - mean * mean
        spread = jnp.sqrt(jnp.maximum(variance, var_floor))
        normed = (value - mean) / spread
        gating_s[rows(q), :] = 1.0 / (1.0 + jnp.exp(-(gate_gain * normed + gate_bias)))
        spread_s[rows(q), :] = spread
        fill_stack(q, normed)
        return carry

    lax.fori_loop(0, 16, normalize, 0, unroll=4)
    arrived(xbuf.at[pl.ds(0, 14)], 3)
    core_blocks = fbuf.at[:, pl.ds(2 * core, 2)]
    copy = swap(core_blocks, core_blocks, 5)
    real, imag = forward()
    spec_x[0], spec_x[1] = real, imag
    copy.wait()

    def take_filter(q, carry):
        fill_stack(q, pair_rows(f_lin, q))
        return carry

    lax.fori_loop(0, 16, take_filter, 0, unroll=2)
    real, imag = forward()
    factor = 1.0 / math.sqrt(LENGTH) / LENGTH
    real, imag = real * factor, imag * factor
    copies = []

    def exchange(half, value):
        place = pl.ds(half * HALF, HALF)
        ybuf[place, :] = value
        copies.append(swap(ybuf.at[place], ygot.at[place], 6 + 9 * half))

    inverse(
        spec_x[0] * real - spec_x[1] * imag, spec_x[0] * imag + spec_x[1] * real, exchange
    )

    loss_acc[...] = jnp.zeros((8, LANES), f32)

    def predict(q, carry):
        value = pair_rows(x_lin, q)
        opening = x_lin[pl.ds(pl.multiple_of(q * 64, 64), 32, stride=2), :][:, 0:1]
        after = jnp.minimum(q * 64 + 64, SHARDS * SEGS - 8)
        following = x_lin[pl.ds(pl.multiple_of(after, 8), 8), :][0:1, 0:1]
        edge = jnp.concatenate([opening[1:], following], axis=0)
        target = jnp.concatenate([value[:, 1:], edge], axis=1)
        weight = spread_s[rows(q), :] * gating_s[rows(q), :]
        predicted = value + weight * (ybuf[rows(q), :] + ygot[rows(q), :])
        put_pairs(p_lin, q, predicted)
        step_index = (q * 32 + row_index) * N2 + lane_index
        residual = jnp.where(step_index < LENGTH - 1, predicted - target, 0.0)
        squares = residual * residual
        squares = squares[:, :LANES] + squares[:, LANES:]
        loss_acc[...] += (squares[0:8] + squares[8:16]) + (squares[16:24] + squares[24:32])
        fill_stack(q, (2.0 / CHANNELS) * residual * weight)
        return carry

    copies[0].wait()
    lax.fori_loop(0, 8, predict, 0, unroll=4)
    copies[1].wait()
    lax.fori_loop(8, 16, predict, 0, unroll=4)

    loss_own[...] = jnp.sum(loss_acc[...], axis=0, keepdims=True)

    def send_loss(step, carry):
        deliver(loss_own, loss_mid.at[plane], 8, 2 * ((plane + step) % 8) + core, at)
        return carry

    lax.fori_loop(0, 8, send_loss, 0)

    for far in FAR_FIRST:
        for side in (2, 1, 3, 0):
            to = 4 * ((depth + far) % 8) + (width + side) % 4
            deliver_far(
                far + side, pbuf.at[to, own_half], pred_out.at[owner_row, own_half], 7,
                2 * plane + owner_core, to,
            )

    real, imag = forward()
    across_r = (real * spec_x[0] + imag * spec_x[1]) * factor
    across_i = (imag * spec_x[0] - real * spec_x[1]) * factor
    copies = []

    def exchange_grad(half, value):
        base, place = half * N1, pl.ds(half * 4, 4)
        c_lin[pl.ds(base, HALF, stride=2), :] = value[:, :LANES]
        c_lin[pl.ds(base + 1, HALF, stride=2), :] = value[:, LANES:]
        copies.append(swap(cbuf.at[place, pl.ds(2 * (1 - core), 2)], cgot.at[place], 9 + 7 * half))

    inverse(across_r, across_i, exchange_grad)

    for half in (0, 1):
        copies[half].wait()
        place = pl.ds(half * 4, 4)
        csum[place] = cbuf[place, pl.ds(2 * core, 2)] + cgot[place]
        for far in FAR_FIRST:
            to = (plane + far) % 8
            piece = pl.ds(pl.multiple_of((to // 2) * 8, 8), 8)
            deliver_far(
                far, csum.at[place, to % 2, piece], along_y.at[half, plane], 11 + 6 * half, 2 * to + core, at
            )

    arrived(loss_mid, 8)
    loss_sum[...] = jnp.sum(loss_mid[...], axis=0)

    def send_loss_sum(step, carry):
        deliver(loss_sum, loss_all.at[at], 10, group, (at + step) % 32)
        return carry

    lax.fori_loop(0, 32, send_loss_sum, 0)

    for half in (0, 1):
        arrived(along_y.at[half], 11 + 6 * half)
        along_sum[pl.ds(half * 4, 4)] = jnp.sum(along_y[half], axis=0)
        for step in range(half * 4, half * 4 + 4):
            deliver(
                along_sum.at[step], across.at[owner_row // 2, owner_core], 12,
                2 * plane + row_odd, 4 * step + 2 * core + on_plane,
            )

    @pl.when(active)
    def _():
        arrived(across, 12)
        across_sum[...] = across[:, 0] + across[:, 1]

        for far in FAR_FIRST:
            deliver_far(
                far, across_sum, grad_out.at[:, core, own_piece], 13, 2 * ((plane + far) % 8) + core, at
            )

    arrived(loss_all, 10)
    everything = jnp.sum(jnp.sum(loss_all[...], axis=0), keepdims=True)
    loss_out[...] = everything / (CHANNELS * (LENGTH - 1))

    arrived(grad_out.at[:, core], 13)
    copy = swap(grad_out.at[:, core], grad_out.at[:, core], 14)

    def drain(less, whole, part, number):
        @pl.when(less)
        def _():
            sent(part, number)

        @pl.when(jnp.logical_not(less))
        def _():
            sent(whole, number)

    own_core = owner_core == core
    drain(own_core, xbuf.at[:, pl.ds(0, 16)], xbuf.at[pl.ds(0, 31), pl.ds(0, 16)], 0)

    @pl.when(active)
    def _():
        drain(
            jnp.logical_and(own_core, row_odd == core),
            xbuf.at[pl.ds(0, 16), pl.ds(0, 8)], xbuf.at[pl.ds(0, 15), pl.ds(0, 8)], 2,
        )
        sent(xbuf.at[pl.ds(0, 14)], 13)

    sent(xbuf.at[pl.ds(0, 14)], 3)
    drain(own_core, xbuf.at[:, pl.ds(0, 16)], xbuf.at[pl.ds(0, 31), pl.ds(0, 16)], 7)
    sent(loss_mid.at[pl.ds(0, 7)], 8)
    sent(loss_all.at[pl.ds(0, 31)], 10)
    sent(xbuf.at[pl.ds(0, 7)], 11)
    sent(xbuf.at[pl.ds(0, 7)], 17)
    drain(
        jnp.logical_and(active, row_odd == core), along_sum, along_sum.at[pl.ds(0, 7)], 12
    )
    arrived(pred_out, 7)
    copy.wait()


def per_device(signal, filters, gate_scale, gate_shift):
    (outer_h, outer_l), (outer_th, outer_tl), (inner_h, inner_l), twist, lane = make_tables()
    vmem = pl.BlockSpec(memory_space=pltpu.VMEM)
    anywhere = pl.BlockSpec(memory_space=pl.ANY)

    def space(*shape, kind=f32):
        return pltpu.VMEM(shape, kind)

    predicted, grad, loss = pl.pallas_call(
        kernel,
        out_shape=(
            pltpu.VMEM((16, SEGS, LANES), f32),
            pltpu.VMEM((8, 2, SEGS, LANES), f32),
            pltpu.VMEM((1, 1), f32),
        ),
        in_specs=[anywhere] * 12,
        out_specs=(vmem, vmem, vmem),
        scratch_shapes=[
            space(16, 4096), space(16, 1024), space(1, 16), space(1, 16), space(8, N2),
            space(512, LANES), space(128, LANES), space(8, LANES), space(8, LANES),
            space(SHARDS, SEGS, LANES), space(8, 4, SEGS, LANES), space(SHARDS, SEGS, LANES),
            space(N1, N2), space(N1, N2), space(8, 4, SEGS, LANES), space(8, 2, SEGS, LANES),
            space(8, 2, SEGS, LANES), space(2, 8, 4, 8, LANES), space(8, 8, LANES),
            space(8, 2, 8, LANES), space(8, 8, LANES),
            space(8, LANES), space(1, LANES), space(8, 1, LANES), space(1, LANES), space(32, 1, LANES),
            space(N1, 3 * N1, kind=bf16), space(N1, 3 * N1, kind=bf16), space(3 * N2, 2 * N2, kind=bf16),
            space(2, HALF, N2),
            space(3 * N1, N2, kind=bf16), space(3 * N1, N2, kind=bf16),
            space(N2, N2, kind=bf16), space(N1, N1, kind=bf16), space(N1, N2),
            space(N1, N2), space(N1, N2), space(N1, N2), space(3 * N1, N2, kind=bf16),
            space(N1, 3 * N2, kind=bf16), space(2, HALF, N2),
            pltpu.SemaphoreType.DMA((15,)), pltpu.SemaphoreType.DMA((18,)), pltpu.SemaphoreType.DMA((18,)),
        ],
        compiler_params=pltpu.CompilerParams(has_side_effects=True, collective_id=1),
    )(
        signal, filters, gate_scale.reshape(1, 16), gate_shift.reshape(1, 16),
        outer_h, outer_l, outer_th, outer_tl, inner_h, inner_l, twist, lane,
    )
    return (predicted.reshape(16, 4096), grad.reshape(16, 4096), loss.reshape(()))


def solution(mesh):
    return jax.shard_map(
        per_device,
        mesh=mesh,
        in_specs=(P("chan", "tm"), P(None, "tm"), P("chan"), P("chan")),
        out_specs=(P("chan", "tm"), P(None, "tm"), P()),
        check_vma=False,
    )
```

```python
import math

import jax
import jax.numpy as jnp
import numpy as np
from jax import lax
from jax.experimental import pallas as pl
from jax.experimental.pallas import tpu as pltpu
from jax.sharding import PartitionSpec as P

CHANNELS = 256
LENGTH = 131072
N1, N2 = 512, 256
HALF = 256
SHARDS = 32
SEGS = 32
LANES = 128
var_floor = 1.0
MESH = pl.DeviceIdType.MESH
FAR_FIRST = (4, 3, 5, 2, 6, 1, 7, 0)
f32, bf16 = jnp.float32, jnp.bfloat16


def split_table(table):
    high = table.astype(np.float32).astype(bf16)
    low = (table - np.asarray(high).astype(np.float64)).astype(np.float32).astype(bf16)
    return np.asarray(high), np.asarray(low)


def make_tables():
    n1, n2 = np.arange(N1), np.arange(N2)
    k1 = np.arange(HALF)
    angle = 2 * math.pi * ((np.outer(4 * k1 + 1, n1) % (4 * N1)) / (4 * N1))
    outer = np.concatenate([np.cos(angle), -np.sin(angle)], axis=0)
    angle = 2 * math.pi * ((np.outer(n2, n2) % N2) / N2)
    inner = np.concatenate([np.cos(angle), np.sin(angle)], axis=1)
    angle = 2 * math.pi * (np.outer(4 * k1 + 1, n2) / (4 * LENGTH))
    twist = np.stack([np.cos(angle), -np.sin(angle)]).astype(np.float32)
    angle = math.pi * n2 / 256
    lane = np.zeros((8, N2), np.float32)
    lane[0], lane[1] = np.cos(angle), -np.sin(angle)
    return split_table(outer), split_table(outer.T), split_table(inner), twist, lane


def high_low(value):
    high = value.astype(bf16)
    return high, (value - high.astype(f32)).astype(bf16)


def three_way(value):
    high = value.astype(bf16)
    rest = value - high.astype(f32)
    middle = rest.astype(bf16)
    return high, middle, (rest - middle.astype(f32)).astype(bf16)


def dot(first, second):
    return jnp.dot(first, second, preferred_element_type=f32)


def kernel(
    signal_hbm, filters_hbm, scale_hbm, shift_hbm,
    outer_h, outer_l, outer_th, outer_tl, inner_h, inner_l, twist_hbm, lane_hbm,
    pred_out, grad_out, loss_out,
    signal, filters, scale_in, shift_in, lane_ref, signal_send, filter_send, gate_send, gate_got,
    xbuf, fbuf, pbuf, ybuf, ygot, cbuf, cgot, csum, along_y, along_sum, across, across_sum,
    loss_acc, loss_own, loss_mid, loss_sum, loss_all,
    outer_k, outer_tk, inner_k, twist,
    triple_x, triple_q, tri_up, tri_low, totals,
    spread_s, normed_s, gating_s, stack, left, spec_x,
    table_sem, send_sem, recv_sem,
):
    group, at = lax.axis_index("chan"), lax.axis_index("tm")
    plane, core = group // 2, group % 2
    owner_core, owner_row = at % 2, at // 2
    depth, width = at // 4, at % 4
    partner = 2 * plane + 1 - core
    own_half = pl.ds(pl.multiple_of(core * 16, 16), 16)
    own_piece = pl.ds(pl.multiple_of((plane // 2) * 8, 8), 8)
    on_plane = plane % 2
    active = at % 2 == on_plane
    row_odd = owner_row % 2

    barrier = pltpu.get_barrier_semaphore()

    def greet(chan, tm):
        pl.semaphore_signal(barrier, inc=1, device_id=(chan, tm), device_id_type=MESH)

    for far in FAR_FIRST[:-1]:
        for step in range(8):
            greet(2 * plane + step % 2, 4 * ((depth + far) % 8) + step // 2)
    for far in FAR_FIRST[:-1]:
        greet(2 * ((plane + far) % 8) + core, at)
    for side in (2, 1, 3):
        for step in (0, 1):
            greet(2 * plane + step, 4 * depth + (width + side) % 4)
    greet(partner, at)

    def fetch(source, target, number):
        return pltpu.make_async_copy(source, target, table_sem.at[number])

    tables = [
        (outer_h, outer_k.at[:, pl.ds(0, N1)]), (outer_h, outer_k.at[:, pl.ds(N1, N1)]),
        (outer_l, outer_k.at[:, pl.ds(2 * N1, N1)]),
        (outer_th, outer_tk.at[:, pl.ds(0, N1)]), (outer_th, outer_tk.at[:, pl.ds(N1, N1)]),
        (outer_tl, outer_tk.at[:, pl.ds(2 * N1, N1)]),
        (inner_h, inner_k.at[pl.ds(0, N2)]), (inner_h, inner_k.at[pl.ds(N2, N2)]),
        (inner_l, inner_k.at[pl.ds(2 * N2, N2)]),
        (twist_hbm, twist), (lane_hbm, lane_ref), (scale_hbm, scale_in), (shift_hbm, shift_in),
    ]
    own_taps = pl.ds(pl.multiple_of((plane // 2) * 1024, 1024), 1024)
    inputs = [(signal_hbm, signal), (filters_hbm.at[:, own_taps], filters)]
    for number, (source, target) in enumerate(inputs):
        fetch(source, target, 13 + number).start()
    for number, (source, target) in enumerate(tables):
        fetch(source, target, number).start()

    def remote(source, target, number, chan, tm):
        return pltpu.make_async_remote_copy(
            src_ref=source, dst_ref=target, send_sem=send_sem.at[number], recv_sem=recv_sem.at[number],
            device_id=(chan, tm), device_id_type=MESH,
        )

    def deliver(source, target, number, chan, tm):
        here = jnp.logical_and(chan == group, tm == at)

        @pl.when(jnp.logical_not(here))
        def _():
            remote(source, target, number, chan, tm).start()

        @pl.when(here)
        def _():
            pltpu.make_async_copy(source, target, recv_sem.at[number]).start()

    def deliver_far(far, source, target, number, chan, tm):
        if far:
            remote(source, target, number, chan, tm).start()
        else:
            deliver(source, target, number, chan, tm)

    def arrived(target, number):
        pltpu.make_async_copy(target, target, recv_sem.at[number]).wait()

    def sent(source, number):
        pltpu.make_async_copy(source, source, send_sem.at[number]).wait()

    def swap(source, target, number):
        copy = remote(source, target, number, partner, at)
        copy.start()
        return copy

    def signal_turn(seg, carry):
        signal_send[pl.ds(seg, 16, stride=SEGS), :] = signal[:, pl.ds(pl.multiple_of(seg * LANES, LANES), LANES)]
        return carry

    fetch(*inputs[0], 13).wait()
    lax.fori_loop(0, SEGS, signal_turn, 0, unroll=4)
    signal_rows = signal_send.reshape(16, SEGS, LANES)
    fetch(*inputs[1], 14).wait()
    for seg in range(8):
        filter_send[pl.ds(seg, 16, stride=8), :] = filters[:, seg * LANES : (seg + 1) * LANES]
    filter_rows = filter_send.reshape(16, 8, LANES)

    pl.semaphore_wait(barrier, 2 * SHARDS - 1 + 7)

    @pl.when(active)
    def _():
        for far in FAR_FIRST:
            for side in (0, 1):
                row = 2 * ((depth + far) % 8) + side
                deliver_far(
                    far, filter_rows.at[row], fbuf.at[depth, width, own_piece], 2,
                    2 * plane + row_odd, 2 * row + core,
                )

    for far in FAR_FIRST:
        for side in (0, 1):
            row = 2 * ((depth + far) % 8) + side
            for half in (0, 1):
                part = pl.ds(half * 16, 16)
                deliver_far(
                    far, signal_rows.at[row, part], xbuf.at[at, part], 0, 2 * plane + half, 2 * row + core
                )
    row_up = lax.broadcasted_iota(jnp.int32, (N2, N2), 0)
    col_up = lax.broadcasted_iota(jnp.int32, (N2, N2), 1)
    tri_up[...] = jnp.where(row_up <= col_up, 1.0, 0.0).astype(bf16)

    def rows(q, offset=0):
        return pl.ds(pl.multiple_of(q * 32 + offset, 32), 32)

    row_low = lax.broadcasted_iota(jnp.int32, (32, N1), 0)
    col_low = lax.broadcasted_iota(jnp.int32, (32, N1), 1)

    def fill_low(q, carry):
        tri_low[rows(q), :] = jnp.where(col_low < row_low + q * 32, 1.0, 0.0).astype(bf16)
        return carry

    lax.fori_loop(0, 16, fill_low, 0)

    for number, (source, target) in enumerate(tables):
        fetch(source, target, number).wait()
    gate_send[...] = jnp.zeros((8, LANES), f32)
    gate_send[0:1, 0:16] = scale_in[...]
    gate_send[1:2, 0:16] = shift_in[...]
    gates = swap(gate_send, gate_got, 1)
    core_f = core.astype(f32)
    lane_r = 1.0 + core_f * (lane_ref[0:1, :] - 1.0)
    lane_i = core_f * lane_ref[1:2, :]
    base_r, base_i = twist[0], twist[1]
    twist[0] = base_r * lane_r - base_i * lane_i
    twist[1] = base_r * lane_i + base_i * lane_r

    rows_here = lax.broadcasted_iota(jnp.int32, (32, 1), 0)
    flip = 1.0 - 2.0 * core_f * (rows_here % 2).astype(f32)
    half_rows = lax.broadcasted_iota(jnp.int32, (HALF, 1), 0)
    flip_half = 1.0 - 2.0 * core_f * (half_rows % 2).astype(f32)

    x_lin = xbuf.reshape(SHARDS * SEGS, LANES)
    f_lin = fbuf.reshape(SHARDS * SEGS, LANES)
    p_lin = pbuf.reshape(SHARDS * SEGS, LANES)
    c_lin = cbuf.reshape(SHARDS * SEGS, LANES)

    def pair_rows(ref, q):
        base = pl.multiple_of(q * 64, 64)
        return jnp.concatenate(
            [ref[pl.ds(base, 32, stride=2), :], ref[pl.ds(base + 1, 32, stride=2), :]], axis=1
        )

    def put_pairs(ref, q, value):
        base = pl.multiple_of(q * 64, 64)
        ref[pl.ds(base, 32, stride=2), :] = value[:, :LANES]
        ref[pl.ds(base + 1, 32, stride=2), :] = value[:, LANES:]

    def fill_stack(q, value):
        high, low = high_low(value * flip)
        stack[rows(q), :] = high
        stack[rows(q, N1), :] = low
        stack[rows(q, 2 * N1), :] = high

    def fill_left(real, imag):
        for part, value in enumerate((real, imag)):
            high, low = high_low(value)
            place = slice(part * HALF, (part + 1) * HALF)
            left[place, 0:N2] = high
            left[place, N2 : 2 * N2] = low
            left[place, 2 * N2 : 3 * N2] = high

    def forward():
        first = dot(outer_k[...], stack[...])
        first_r, first_i = first[:HALF], first[HALF:]
        fill_left(first_r * twist[0] - first_i * twist[1], first_r * twist[1] + first_i * twist[0])
        quads = dot(left[...], inner_k[...])
        return quads[:HALF, :N2] + quads[HALF:, N2:], quads[HALF:, :N2] - quads[:HALF, N2:]

    def inverse(real, imag, take):
        fill_left(real, imag)
        quads = dot(left[...], inner_k[...])
        mid_r = quads[:HALF, :N2] - quads[HALF:, N2:]
        mid_i = quads[HALF:, :N2] + quads[:HALF, N2:]
        high, low = high_low(mid_r * twist[0] + mid_i * twist[1])
        stack[0:HALF, :] = high
        stack[N1 : N1 + HALF, :] = low
        stack[2 * N1 : 2 * N1 + HALF, :] = high
        high, low = high_low(mid_i * twist[0] - mid_r * twist[1])
        stack[HALF:N1, :] = high
        stack[N1 + HALF : 2 * N1, :] = low
        stack[2 * N1 + HALF : 3 * N1, :] = high
        for half in (0, 1):
            place = slice(half * HALF, (half + 1) * HALF)
            take(half, dot(outer_tk[place, :], stack[...]) * flip_half)

    own_blocks = fbuf.at[:, 2 * core + on_plane, own_piece]
    arrived(own_blocks, 2)

    for far in FAR_FIRST[:-1]:
        remote(own_blocks, own_blocks, 3, 2 * ((plane + far) % 8) + core, at).start()
    arrived(xbuf.at[:, own_half], 0)
    copy = swap(xbuf.at[:, own_half], xbuf.at[:, own_half], 4)
    copy.wait()

    def split_rows(q, carry):
        value = pair_rows(x_lin, q)
        for part, piece in enumerate(three_way(value)):
            triple_x[rows(q, part * N1), :] = piece
        for part, piece in enumerate(three_way(value * value)):
            triple_q[rows(q, part * N1), :] = piece
        return carry

    lax.fori_loop(0, 16, split_rows, 0, unroll=2)
    sums = dot(triple_x[...], tri_up[...])
    normed_s[...] = sums[:N1] + sums[N1 : 2 * N1] + sums[2 * N1 :]
    sums = dot(triple_q[...], tri_up[...])
    spread_s[...] = sums[:N1] + sums[N1 : 2 * N1] + sums[2 * N1 :]
    row_sums = jnp.concatenate(
        [
            jnp.broadcast_to(normed_s[:, N2 - 1 : N2], (N1, LANES)),
            jnp.broadcast_to(spread_s[:, N2 - 1 : N2], (N1, LANES)),
        ],
        axis=1,
    )
    carried = dot(tri_low[...], jnp.concatenate(three_way(row_sums), axis=1))
    totals[...] = carried[:, :N2] + carried[:, N2 : 2 * N2] + carried[:, 2 * N2 :]

    gates.wait()
    gate_pair = jnp.where(core == owner_core, gate_send[...], gate_got[...])
    pick = lax.broadcasted_iota(jnp.int32, (1, LANES), 1) == owner_row
    gate_gain = jnp.sum(jnp.where(pick, gate_pair[0:1, :], 0.0), axis=1, keepdims=True)
    gate_bias = jnp.sum(jnp.where(pick, gate_pair[1:2, :], 0.0), axis=1, keepdims=True)

    lane_index = lax.broadcasted_iota(jnp.int32, (32, N2), 1)
    row_index = lax.broadcasted_iota(jnp.int32, (32, N2), 0)

    def normalize(q, carry):
        value = pair_rows(x_lin, q)
        before = totals[rows(q), :]
        first = normed_s[rows(q), :] + jnp.concatenate([before[:, :LANES]] * 2, axis=1)
        second = spread_s[rows(q), :] + jnp.concatenate([before[:, LANES:]] * 2, axis=1)
        counts = ((q * 32 + row_index) * N2 + lane_index + 1).astype(f32)
        mean = first / counts
        variance = second / counts - mean * mean
        spread = jnp.sqrt(jnp.maximum(variance, var_floor))
        normed = (value - mean) / spread
        gating_s[rows(q), :] = 1.0 / (1.0 + jnp.exp(-(gate_gain * normed + gate_bias)))
        spread_s[rows(q), :] = spread
        fill_stack(q, normed)
        return carry

    lax.fori_loop(0, 16, normalize, 0, unroll=4)
    arrived(xbuf.at[pl.ds(0, 14)], 3)
    core_blocks = fbuf.at[:, pl.ds(2 * core, 2)]
    copy = swap(core_blocks, core_blocks, 5)
    real, imag = forward()
    spec_x[0], spec_x[1] = real, imag
    copy.wait()

    def take_filter(q, carry):
        fill_stack(q, pair_rows(f_lin, q))
        return carry

    lax.fori_loop(0, 16, take_filter, 0, unroll=2)
    real, imag = forward()
    factor = 1.0 / math.sqrt(LENGTH) / LENGTH
    real, imag = real * factor, imag * factor
    copies = []

    def exchange(half, value):
        place = pl.ds(half * HALF, HALF)
        ybuf[place, :] = value
        copies.append(swap(ybuf.at[place], ygot.at[place], 6 + 9 * half))

    inverse(
        spec_x[0] * real - spec_x[1] * imag, spec_x[0] * imag + spec_x[1] * real, exchange
    )

    loss_acc[...] = jnp.zeros((8, LANES), f32)

    def predict(q, carry):
        value = pair_rows(x_lin, q)
        opening = x_lin[pl.ds(pl.multiple_of(q * 64, 64), 32, stride=2), :][:, 0:1]
        after = jnp.minimum(q * 64 + 64, SHARDS * SEGS - 8)
        following = x_lin[pl.ds(pl.multiple_of(after, 8), 8), :][0:1, 0:1]
        edge = jnp.concatenate([opening[1:], following], axis=0)
        target = jnp.concatenate([value[:, 1:], edge], axis=1)
        weight = spread_s[rows(q), :] * gating_s[rows(q), :]
        predicted = value + weight * (ybuf[rows(q), :] + ygot[rows(q), :])
        put_pairs(p_lin, q, predicted)
        step_index = (q * 32 + row_index) * N2 + lane_index
        residual = jnp.where(step_index < LENGTH - 1, predicted - target, 0.0)
        squares = residual * residual
        squares = squares[:, :LANES] + squares[:, LANES:]
        loss_acc[...] += (squares[0:8] + squares[8:16]) + (squares[16:24] + squares[24:32])
        fill_stack(q, (2.0 / CHANNELS) * residual * weight)
        return carry

    copies[0].wait()
    lax.fori_loop(0, 8, predict, 0, unroll=4)
    copies[1].wait()
    lax.fori_loop(8, 16, predict, 0, unroll=4)

    loss_own[...] = jnp.sum(loss_acc[...], axis=0, keepdims=True)

    def send_loss(step, carry):
        deliver(loss_own, loss_mid.at[plane], 8, 2 * ((plane + step) % 8) + core, at)
        return carry

    lax.fori_loop(0, 8, send_loss, 0)

    for far in FAR_FIRST:
        for side in (2, 1, 3, 0):
            to = 4 * ((depth + far) % 8) + (width + side) % 4
            deliver_far(
                far + side, pbuf.at[to, own_half], pred_out.at[owner_row, own_half], 7,
                2 * plane + owner_core, to,
            )

    real, imag = forward()
    across_r = (real * spec_x[0] + imag * spec_x[1]) * factor
    across_i = (imag * spec_x[0] - real * spec_x[1]) * factor
    copies = []

    def exchange_grad(half, value):
        base, place = half * N1, pl.ds(half * 4, 4)
        c_lin[pl.ds(base, HALF, stride=2), :] = value[:, :LANES]
        c_lin[pl.ds(base + 1, HALF, stride=2), :] = value[:, LANES:]
        copies.append(swap(cbuf.at[place, pl.ds(2 * (1 - core), 2)], cgot.at[place], 9 + 7 * half))

    inverse(across_r, across_i, exchange_grad)

    for half in (0, 1):
        copies[half].wait()
        place = pl.ds(half * 4, 4)
        csum[place] = cbuf[place, pl.ds(2 * core, 2)] + cgot[place]
        for far in FAR_FIRST:
            to = (plane + far) % 8
            piece = pl.ds(pl.multiple_of((to // 2) * 8, 8), 8)
            deliver_far(
                far, csum.at[place, to % 2, piece], along_y.at[half, plane], 11 + 6 * half, 2 * to + core, at
            )

    arrived(loss_mid, 8)
    loss_sum[...] = jnp.sum(loss_mid[...], axis=0)

    def send_loss_sum(step, carry):
        deliver(loss_sum, loss_all.at[at], 10, group, (at + step) % 32)
        return carry

    lax.fori_loop(0, 32, send_loss_sum, 0)

    for half in (0, 1):
        arrived(along_y.at[half], 11 + 6 * half)
        along_sum[pl.ds(half * 4, 4)] = jnp.sum(along_y[half], axis=0)
        for step in range(half * 4, half * 4 + 4):
            deliver(
                along_sum.at[step], across.at[owner_row // 2, owner_core], 12,
                2 * plane + row_odd, 4 * step + 2 * core + on_plane,
            )

    @pl.when(active)
    def _():
        arrived(across, 12)
        across_sum[...] = across[:, 0] + across[:, 1]
        own_sem = 18 + plane // 2

        for far in FAR_FIRST:
            deliver_far(
                far, across_sum, grad_out.at[:, core, own_piece], own_sem, 2 * ((plane + far) % 8) + core, at
            )

    arrived(loss_all, 10)
    everything = jnp.sum(jnp.sum(loss_all[...], axis=0), keepdims=True)
    loss_out[...] = everything / (CHANNELS * (LENGTH - 1))

    forwarded = []
    for piece in range(4):
        place = grad_out.at[:, core, pl.ds(8 * piece, 8)]
        arrived(place, 18 + piece)
        forwarded.append(swap(place, place, 22 + piece))

    def drain(less, whole, part, number):
        @pl.when(less)
        def _():
            sent(part, number)

        @pl.when(jnp.logical_not(less))
        def _():
            sent(whole, number)

    own_core = owner_core == core
    own_sem_all = 18 + plane // 2
    drain(own_core, xbuf.at[:, pl.ds(0, 16)], xbuf.at[pl.ds(0, 31), pl.ds(0, 16)], 0)

    @pl.when(active)
    def _():
        drain(
            jnp.logical_and(own_core, row_odd == core),
            xbuf.at[pl.ds(0, 16), pl.ds(0, 8)], xbuf.at[pl.ds(0, 15), pl.ds(0, 8)], 2,
        )
        sent(xbuf.at[pl.ds(0, 14)], own_sem_all)

    sent(xbuf.at[pl.ds(0, 14)], 3)
    drain(own_core, xbuf.at[:, pl.ds(0, 16)], xbuf.at[pl.ds(0, 31), pl.ds(0, 16)], 7)
    sent(loss_mid.at[pl.ds(0, 7)], 8)
    sent(loss_all.at[pl.ds(0, 31)], 10)
    sent(xbuf.at[pl.ds(0, 7)], 11)
    sent(xbuf.at[pl.ds(0, 7)], 17)
    drain(
        jnp.logical_and(active, row_odd == core), along_sum, along_sum.at[pl.ds(0, 7)], 12
    )
    arrived(pred_out, 7)
    for copy in forwarded:
        copy.wait()


def per_device(signal, filters, gate_scale, gate_shift):
    (outer_h, outer_l), (outer_th, outer_tl), (inner_h, inner_l), twist, lane = make_tables()
    vmem = pl.BlockSpec(memory_space=pltpu.VMEM)
    anywhere = pl.BlockSpec(memory_space=pl.ANY)

    def space(*shape, kind=f32):
        return pltpu.VMEM(shape, kind)

    predicted, grad, loss = pl.pallas_call(
        kernel,
        out_shape=(
            pltpu.VMEM((16, SEGS, LANES), f32),
            pltpu.VMEM((8, 2, SEGS, LANES), f32),
            pltpu.VMEM((1, 1), f32),
        ),
        in_specs=[anywhere] * 12,
        out_specs=(vmem, vmem, vmem),
        scratch_shapes=[
            space(16, 4096), space(16, 1024), space(1, 16), space(1, 16), space(8, N2),
            space(512, LANES), space(128, LANES), space(8, LANES), space(8, LANES),
            space(SHARDS, SEGS, LANES), space(8, 4, SEGS, LANES), space(SHARDS, SEGS, LANES),
            space(N1, N2), space(N1, N2), space(8, 4, SEGS, LANES), space(8, 2, SEGS, LANES),
            space(8, 2, SEGS, LANES), space(2, 8, 4, 8, LANES), space(8, 8, LANES),
            space(8, 2, 8, LANES), space(8, 8, LANES),
            space(8, LANES), space(1, LANES), space(8, 1, LANES), space(1, LANES), space(32, 1, LANES),
            space(N1, 3 * N1, kind=bf16), space(N1, 3 * N1, kind=bf16), space(3 * N2, 2 * N2, kind=bf16),
            space(2, HALF, N2),
            space(3 * N1, N2, kind=bf16), space(3 * N1, N2, kind=bf16),
            space(N2, N2, kind=bf16), space(N1, N1, kind=bf16), space(N1, N2),
            space(N1, N2), space(N1, N2), space(N1, N2), space(3 * N1, N2, kind=bf16),
            space(N1, 3 * N2, kind=bf16), space(2, HALF, N2),
            pltpu.SemaphoreType.DMA((15,)), pltpu.SemaphoreType.DMA((26,)), pltpu.SemaphoreType.DMA((26,)),
        ],
        compiler_params=pltpu.CompilerParams(has_side_effects=True, collective_id=1),
    )(
        signal, filters, gate_scale.reshape(1, 16), gate_shift.reshape(1, 16),
        outer_h, outer_l, outer_th, outer_tl, inner_h, inner_l, twist, lane,
    )
    return (predicted.reshape(16, 4096), grad.reshape(16, 4096), loss.reshape(()))


def solution(mesh):
    return jax.shard_map(
        per_device,
        mesh=mesh,
        in_specs=(P("chan", "tm"), P(None, "tm"), P("chan"), P("chan")),
        out_specs=(P("chan", "tm"), P(None, "tm"), P()),
        check_vma=False,
    )
```
